128 devices in a mesh: rep: 8 (over y, x_lo), seq: 16 (over z, x_hi, core).
Axes of the slice: x: 4 (x_hi: 2, x_lo: 2; x = x_hi * 2 + x_lo), y: 4, z: 4, core: 2. Of those that a mesh axis runs over, the one named last changes fastest.
Arguments:
- features: float32 [8, 3, 64, 65536], P('rep', None, None, 'seq'), may hold values from -6 to 6
- short_filter: float32 [3, 3, 64], replicated, may hold values from -3 to 3
- long_filter: float32 [64, 65536], P('seq', 'rep'), may hold values from -4 to 4
- skip_gain: float32 [64], P('seq'), may hold values from -4 to 4
- lengths: int32 [8], P('rep'), may hold values from 1 to 65536, as said below
Outputs:
- mixed: float32 [8, 64, 65536], P('rep', None, 'seq')
The draws below stay inside these ranges and needn't reach their ends.
Inputs may be any that keep to these rules, and one draw needn't show every extreme that they name: `lengths`: one replica's length is exactly 65536.
All inputs are finite; a program needn't handle non-finite values.
Results may differ from the reference program's by a relative error of at most 0.00012.
Values sent between devices are 32-bit elements; how exact they have to be, the bound alone decides.
No kernel may reach another device: no remote copies, remote signals or barrier semaphores. Data moves between devices by JAX's collectives and lax.ppermute only.
A program may use at most 320 MiB of HBM per device.

```python
import jax
import jax.numpy as jnp
from jax import lax

CH = 64
LMAX = 65536
REPS = 8


def envelope_norm(rate, count):
    return jnp.sqrt(jnp.expm1(-2.0 * rate * count) / jnp.expm1(-2.0 * rate))


def draw_long_filter(key, part):
    noise_key = jax.random.fold_in(jax.random.fold_in(key, 11), 0)
    slow_key = jax.random.fold_in(jax.random.fold_in(key, 11), 3)
    tail_key = jax.random.fold_in(jax.random.fold_in(key, 11), 4)
    tail_rate_key = jax.random.fold_in(jax.random.fold_in(key, 11), 5)
    noise = jax.random.normal(noise_key, (CH, LMAX), jnp.float32)
    tail_noise = jax.random.normal(tail_key, (CH, LMAX), jnp.float32)
    decay = jnp.exp(jax.random.uniform(slow_key, (CH,), jnp.float32, jnp.log(0.5 / LMAX), jnp.log(1.0 / 30.0)))
    base = noise
    tail_base = tail_noise
    positions = jnp.arange(LMAX, dtype=jnp.float32)
    envelope = jnp.exp(-decay[:, None] * positions[None, :])
    head = base * envelope / envelope_norm(decay, LMAX)[:, None]
    tail_rate = jnp.exp(jax.random.uniform(tail_rate_key, (CH,), jnp.float32, jnp.log(0.2 / LMAX), jnp.log(2.0 / LMAX)))
    tail_envelope = jnp.exp(-tail_rate[:, None] * positions[None, :])
    tail = 0.3 * tail_base * tail_envelope / envelope_norm(tail_rate, LMAX)[:, None]
    return jnp.clip(head + tail, -4.0, 4.0)


def draw_lengths(key, part):
    first_key, place_key, other_key, short_key = jax.random.split(jax.random.fold_in(key, 23), 4)
    drawn = jax.random.randint(first_key, (REPS,), 1, LMAX + 1, jnp.int32)
    longest = jax.random.randint(place_key, (), 0, REPS, jnp.int32)
    drawn = drawn.at[longest].set(LMAX)
    second = (longest + 1 + jax.random.randint(other_key, (), 0, REPS - 1, jnp.int32)) % REPS
    drawn = drawn.at[second].set(jax.random.randint(short_key, (), 1, LMAX // 2 + 1, jnp.int32))
    return drawn


def level_of(rng, shape, pieces, smallest, high):
    level = 1.0
    for position, blocks in pieces:
        heights = jax.random.uniform(jax.random.fold_in(jax.random.fold_in(rng, 6), position), (blocks,), jnp.float32, smallest / len(pieces), high / len(pieces))
        level = level * jnp.repeat(jnp.exp(heights), shape[position] // blocks).reshape((-1,) + (1,) * (len(shape) - 1 - position))
    return level


def bell_draw(rng, shape, deviation, limit, shards=(), kind=jnp.bfloat16):
    result = deviation * jax.random.normal(rng, shape, jnp.float32)
    if shards:
        result = result * level_of(rng, shape, shards, -0.22, 0.18)
    return jnp.clip(result, -limit, limit).astype(kind)


def setup_inputs(seed: int = 0) -> dict:
    arg_keys = jax.random.split(jax.random.key(seed), 6)
    return {
        "features": bell_draw(arg_keys[0], (REPS, 3, CH, LMAX), 1.0, 6.0, ((0, 8), (3, 16)), jnp.float32),
        "short_filter": bell_draw(arg_keys[1], (3, 3, CH), 0.6, 3.0, (), jnp.float32),
        "long_filter": draw_long_filter(jax.random.fold_in(arg_keys[5], 71), 0),
        "skip_gain": bell_draw(arg_keys[3], (CH,), 1.0, 4.0, ((0, 16),), jnp.float32),
        "lengths": draw_lengths(jax.random.fold_in(arg_keys[5], 71), 0),
    }


def reference(features, short_filter, long_filter, skip_gain, lengths):
    padded = jnp.pad(features, ((0, 0), (0, 0), (0, 0), (2, 0)))
    featured = short_filter[:, 0, :][None, :, :, None] * padded[..., 2:2 + LMAX]
    featured = featured + short_filter[:, 1, :][None, :, :, None] * padded[..., 1:1 + LMAX]
    featured = featured + short_filter[:, 2, :][None, :, :, None] * padded[..., 0:LMAX]
    positions = jnp.arange(LMAX, dtype=jnp.int32)
    valid = (positions[None, :] < lengths[:, None]).astype(featured.dtype)[:, None, :]
    gated = featured[:, 1] * featured[:, 2] * valid
    fft_size = 2 * LMAX
    filter_spec = jnp.fft.rfft(long_filter, n=fft_size, axis=-1)

    def convolve_one(gated_row):
        spectrum = jnp.fft.rfft(gated_row, n=fft_size, axis=-1) * filter_spec
        return jnp.fft.irfft(spectrum, n=fft_size, axis=-1)[:, :LMAX]

    convolved = lax.map(convolve_one, gated) + skip_gain[None, :, None] * gated
    return featured[:, 0] * convolved * valid
```

```python
import math

import jax
import jax.numpy as jnp
import ml_dtypes
import numpy as np
from jax import lax
from jax.experimental import pallas as pl
from jax.experimental.pallas import tpu as pltpu
from jax.sharding import Mesh
from jax.sharding import PartitionSpec as P

R = 256
N = R * R
BF = jnp.bfloat16
F32 = jnp.float32


def halves(table):
    high = table.astype(np.float32).astype(ml_dtypes.bfloat16)
    low = (table - high.astype(np.float64)).astype(np.float32).astype(ml_dtypes.bfloat16)
    return high, low


def tables():
    row = np.arange(R, dtype=np.float64)
    first = 2.0 * math.pi / R * np.outer(row + 0.25, row)
    outer = np.concatenate([np.cos(first), -np.sin(first)], axis=0)
    twist = 2.0 * math.pi / N * np.outer(row + 0.25, row)
    turn = np.stack([np.cos(twist), -np.sin(twist)]).astype(np.float32)
    last = 2.0 * math.pi / R * np.outer(row, row)
    inner = np.block([[np.cos(last), -np.sin(last)], [np.sin(last), np.cos(last)]])
    outer_high, outer_low = halves(outer)
    back_high, back_low = halves(outer.T.copy())
    inner_high, inner_low = halves(inner)
    inv_high, inv_low = halves(inner.T.copy())
    return (
        np.concatenate([outer_high, outer_low], axis=0),
        np.concatenate([back_high, back_low], axis=0),
        np.concatenate([inner_high, inner_low], axis=0),
        np.concatenate([inv_high, inv_low], axis=0),
        turn,
    )


def split(value):
    high = value.astype(BF)
    return high, (value - high.astype(F32)).astype(BF)


def dot(left, right):
    return jnp.dot(left, right, preferred_element_type=F32)


def wide_dot(left_high, left_low, right_high, right_low):
    return dot(left_high, right_high) + dot(left_low, right_high) + dot(left_high, right_low)


def to_spectrum(signal, outer_ref, inner_ref, turn_ref):
    high, low = split(signal)
    first = wide_dot(outer_ref[0 : 2 * R], outer_ref[2 * R : 4 * R], high, low)
    real, imag = first[0:R], first[R : 2 * R]
    turn_real, turn_imag = turn_ref[0], turn_ref[1]
    turned = jnp.concatenate(
        [real * turn_real - imag * turn_imag, real * turn_imag + imag * turn_real], axis=1
    )
    high, low = split(turned)
    spec = wide_dot(high, low, inner_ref[0 : 2 * R], inner_ref[2 * R : 4 * R])
    return spec[:, 0:R], spec[:, R : 2 * R]


def to_signal(real, imag, back_ref, inv_ref, turn_ref):
    high, low = split(jnp.concatenate([real, imag], axis=1))
    mid = wide_dot(high, low, inv_ref[0 : 2 * R], inv_ref[2 * R : 4 * R])
    real, imag = mid[:, 0:R], mid[:, R : 2 * R]
    turn_real, turn_imag = turn_ref[0], turn_ref[1]
    turned = jnp.concatenate(
        [real * turn_real + imag * turn_imag, imag * turn_real - real * turn_imag], axis=0
    )
    high, low = split(turned)
    return wide_dot(back_ref[0:R], back_ref[R : 2 * R], high, low)


def gate_kernel(length_ref, taps_ref, features_ref, gated_ref, query_ref, column_ref):
    step = pl.program_id(0)
    group = features_ref.shape[2]
    width = features_ref.shape[3]

    @pl.when(step == 0)
    def _():
        taps = jnp.concatenate([taps_ref[j] for j in range(3)], axis=0)
        padded = jnp.concatenate([taps, jnp.zeros((7, taps.shape[1]), F32)], axis=0)
        column_ref[:, 0:16] = padded.T

    limit = length_ref[0] - lax.axis_index("seq") * width
    lane = lax.broadcasted_iota(jnp.int32, (8, width), 1)
    near = lane[:, 0:128]
    for sub in range(group // 8):
        rows = pl.ds(pl.multiple_of(step * group + sub * 8, 8), 8)
        column = column_ref[rows, :]

        def stream(j):
            here = features_ref[0, j, sub * 8 : sub * 8 + 8, :]
            one = pltpu.roll(here, 1, 1)
            two = pltpu.roll(here, 2, 1)
            t0, t1, t2 = (column[:, 3 * j + i : 3 * j + i + 1] for i in range(3))
            value = t0 * here + t1 * jnp.where(lane < 1, 0.0, one) + t2 * jnp.where(lane < 2, 0.0, two)
            over = t1 * jnp.where(near < 1, one[:, 0:128], 0.0) + t2 * jnp.where(
                near < 2, two[:, 0:128], 0.0
            )
            return value, over

        valid = lane < limit
        query, _ = stream(0)
        query_ref[sub * 8 : sub * 8 + 8, :] = jnp.where(valid, query, 0.0)
        key, key_over = stream(1)
        value, value_over = stream(2)
        gated = jnp.where(valid, key * value, 0.0)
        edge = jnp.where(
            near < 2,
            key[:, 0:128],
            jnp.where(
                near < 4,
                pltpu.roll(value[:, 0:128], 2, 1),
                jnp.where(near < 6, pltpu.roll(key_over, 4, 1), pltpu.roll(value_over, 6, 1)),
            ),
        )
        for part in range(2):
            dest = sub * 2 + part
            for tile in range(width // 128):
                place, half = tile // 2, tile % 2
                gated_ref[dest, pl.ds(half * 16 + place, 4, stride=32), :] = gated[
                    4 * part : 4 * part + 4, tile * 128 : tile * 128 + 128
                ]
            gated_ref[dest, 128:132, :] = edge[4 * part : 4 * part + 4]
            gated_ref[dest, 132:136, :] = jnp.zeros((4, 128), F32)


def gate(lengths, short_filter, features):
    _, streams, channels, width = features.shape
    group = 16
    return pl.pallas_call(
        gate_kernel,
        grid=(channels // group,),
        in_specs=[
            pl.BlockSpec(memory_space=pltpu.SMEM),
            pl.BlockSpec(short_filter.shape, lambda i: (0, 0, 0)),
            pl.BlockSpec((1, streams, group, width), lambda i: (0, 0, i, 0)),
        ],
        out_specs=[
            pl.BlockSpec((group // 4, 136, 128), lambda i: (i, 0, 0)),
            pl.BlockSpec((group, width), lambda i: (i, 0)),
        ],
        out_shape=[
            jax.ShapeDtypeStruct((channels // 4, 136, 128), F32),
            jax.ShapeDtypeStruct((channels, width), F32),
        ],
        scratch_shapes=[pltpu.VMEM((channels, 128), F32)],
        compiler_params=pltpu.CompilerParams(vmem_limit_bytes=24 << 20),
        name="gate",
    )(lengths, short_filter, features)


def filter_kernel(skip_ref, filter_ref, outer_ref, inner_ref, turn_ref, spec_ref):
    for channel in range(4):
        taps = jnp.concatenate(
            [filter_ref[y, x, channel] for y in range(4) for x in range(2)], axis=0
        )
        real, imag = to_spectrum(taps, outer_ref, inner_ref, turn_ref)
        spec_ref[channel, 0] = (real + skip_ref[channel]) * (1.0 / N)
        spec_ref[channel, 1] = imag * (1.0 / N)


VM = pl.BlockSpec(memory_space=pltpu.VMEM)
SM = pl.BlockSpec(memory_space=pltpu.SMEM)


def filter_spectrum(skip_gain, filter_parts, consts):
    outer, _, inner, _, turn = consts
    return pl.pallas_call(
        filter_kernel,
        in_specs=[SM, VM, VM, VM, VM],
        out_specs=VM,
        out_shape=jax.ShapeDtypeStruct((4, 2, R, R), F32),
        compiler_params=pltpu.CompilerParams(vmem_limit_bytes=32 << 20),
        name="filter_spectrum",
    )(skip_gain, filter_parts, outer, inner, turn)


def conv_kernel(
    length_ref, moved_ref, spec_ref, outer_ref, back_ref, inner_ref, inv_ref, turn_ref, out_ref, signal_ref
):
    blocks = moved_ref.shape[0]
    width = N // blocks
    lane = lax.broadcasted_iota(jnp.int32, (blocks, 128), 1)
    block = lax.broadcasted_iota(jnp.int32, (blocks, 128), 0)
    inside = (lane < 2) & (block * width + lane < length_ref[0])
    for channel in range(4):
        for half in range(2):
            start = channel * 32 + half * 16
            signal_ref[:, half * 128 : half * 128 + 128] = moved_ref[:, start : start + 16, :].reshape(R, 128)
        edge = jnp.concatenate([moved_ref[b, 128 + channel : 129 + channel, :] for b in range(blocks)], axis=0)
        behind = jnp.where(block < 1, 0.0, pltpu.roll(edge, 1, 0))
        key = edge + pltpu.roll(behind, 124, 1)
        value = pltpu.roll(edge, 126, 1) + pltpu.roll(behind, 122, 1)
        mended = jnp.where(inside, key * value, 0.0)
        for b in range(blocks):
            row = signal_ref[16 * b : 16 * b + 1, 0:128]
            signal_ref[16 * b : 16 * b + 1, 0:128] = jnp.where(lane[0:1] < 2, mended[b : b + 1], row)
        real, imag = to_spectrum(signal_ref[...], outer_ref, inner_ref, turn_ref)
        spec_real, spec_imag = spec_ref[channel, 0], spec_ref[channel, 1]
        result = to_signal(
            real * spec_real - imag * spec_imag,
            real * spec_imag + imag * spec_real,
            back_ref,
            inv_ref,
            turn_ref,
        )
        for half in range(2):
            start = channel * 32 + half * 16
            out_ref[:, start : start + 16, :] = result[:, half * 128 : half * 128 + 128].reshape(blocks, 16, 128)


def convolve(lengths, moved, spec, consts):
    outer, back, inner, inv, turn = consts
    return pl.pallas_call(
        conv_kernel,
        in_specs=[SM] + [VM] * 7,
        out_specs=VM,
        out_shape=jax.ShapeDtypeStruct((moved.shape[0], 128, 128), F32),
        scratch_shapes=[pltpu.VMEM((R, R), F32)],
        compiler_params=pltpu.CompilerParams(vmem_limit_bytes=40 << 20),
        name="convolve",
    )(lengths, moved, spec, outer, back, inner, inv, turn)


def mix_kernel(length_ref, taps_ref, tail_ref, query_ref, back_ref, out_ref):
    group, width = query_ref.shape
    limit = length_ref[0] - lax.axis_index("seq") * width
    lane = lax.broadcasted_iota(jnp.int32, (8, 128), 1)
    for sub in range(group // 8):
        t1 = taps_ref[sub * 8 : sub * 8 + 8, 1:2]
        t2 = taps_ref[sub * 8 : sub * 8 + 8, 2:3]
        far = tail_ref[sub * 8 : sub * 8 + 8, 0:1]
        near = tail_ref[sub * 8 : sub * 8 + 8, 1:2]
        mend = jnp.where(lane == 0, t1 * near + t2 * far, jnp.where(lane == 1, t2 * near, 0.0))
        mend = jnp.where(lane < limit, mend, 0.0)
        for tile in range(width // 128):
            place, half = tile // 2, tile % 2
            query = query_ref[sub * 8 : sub * 8 + 8, tile * 128 : tile * 128 + 128]
            if tile == 0:
                query = query + mend
            parts = [
                back_ref[sub * 2 + part, pl.ds(half * 16 + place, 4, stride=32), :] for part in range(2)
            ]
            out_ref[0, sub * 8 : sub * 8 + 8, tile * 128 : tile * 128 + 128] = query * jnp.concatenate(
                parts, axis=0
            )


def mix(lengths, taps, tail, query, returned):
    channels, width = query.shape
    group = 16
    return pl.pallas_call(
        mix_kernel,
        grid=(channels // group,),
        in_specs=[
            SM,
            pl.BlockSpec((group, 3), lambda i: (i, 0)),
            pl.BlockSpec((group, 2), lambda i: (i, 0)),
            pl.BlockSpec((group, width), lambda i: (i, 0)),
            pl.BlockSpec((group // 4, 128, 128), lambda i: (i, 0, 0)),
        ],
        out_specs=pl.BlockSpec((1, group, width), lambda i: (0, i, 0)),
        out_shape=jax.ShapeDtypeStruct((1, channels, width), F32),
        compiler_params=pltpu.CompilerParams(vmem_limit_bytes=24 << 20),
        name="mix",
    )(lengths, taps, tail, query, returned)


def body(features, short_filter, long_filter, skip_gain, lengths):
    seq_dev = features.shape[3]
    n_seq = lax.axis_size("seq")
    consts = tuple(jnp.asarray(t) for t in tables())
    mine = long_filter.reshape(4, 32, R)
    other = lax.ppermute(mine, "x_lo", [(0, 1), (1, 0)])
    first = lax.axis_index("x_lo") == 0
    pair = jnp.stack([jnp.where(first, mine, other), jnp.where(first, other, mine)])
    filter_parts = lax.all_gather(pair, "y", axis=0, tiled=False)
    gated, query = gate(lengths, short_filter, features)
    moved = lax.all_to_all(gated, "seq", split_axis=0, concat_axis=0, tiled=True)
    tail = lax.ppermute(features[0, 0, :, seq_dev - 2 :], "seq", [(i, i + 1) for i in range(n_seq - 1)])
    spec = filter_spectrum(skip_gain, filter_parts, consts)
    convolved = convolve(lengths, moved, spec, consts)
    returned = lax.all_to_all(convolved, "seq", split_axis=0, concat_axis=0, tiled=True)
    return mix(lengths, short_filter[0].T, tail, query, returned)


def solution(mesh):
    devices = mesh.devices
    reps, seqs = devices.shape
    finer = Mesh(devices.reshape(reps // 2, 2, seqs), ("y", "x_lo", "seq"))
    rep = ("y", "x_lo")
    return jax.shard_map(
        body,
        mesh=finer,
        in_specs=(P(rep, None, None, "seq"), P(), P("seq", rep), P("seq"), P(rep)),
        out_specs=P(rep, None, "seq"),
        check_vma=False,
    )
```

```python
import math

import jax
import jax.numpy as jnp
import ml_dtypes
import numpy as np
from jax import lax
from jax.experimental import pallas as pl
from jax.experimental.pallas import tpu as pltpu
from jax.sharding import Mesh
from jax.sharding import PartitionSpec as P

R = 256
N = R * R
BF = jnp.bfloat16
F32 = jnp.float32
SPAN = 36

VM = pl.BlockSpec(memory_space=pltpu.VMEM)
SM = pl.BlockSpec(memory_space=pltpu.SMEM)
HB = pl.BlockSpec(memory_space=pltpu.HBM)


def halves(table, axis):
    high = table.astype(np.float32).astype(ml_dtypes.bfloat16)
    low = (table - high.astype(np.float64)).astype(np.float32).astype(ml_dtypes.bfloat16)
    return np.concatenate([high, low], axis=axis)


def tables():
    row = np.arange(R, dtype=np.float64)
    first = 2.0 * math.pi / R * np.outer(row + 0.25, row)
    outer = np.concatenate([np.cos(first), -np.sin(first)], axis=0)
    twist = 2.0 * math.pi / N * np.outer(row + 0.25, row)
    turn = np.stack([np.cos(twist), -np.sin(twist)]).astype(np.float32)
    last = 2.0 * math.pi / R * np.outer(row, row)
    inner = np.block([[np.cos(last), -np.sin(last)], [np.sin(last), np.cos(last)]])
    return np.concatenate([halves(outer, 1), halves(outer.T, 0), halves(inner, 0)], axis=0), turn


TABLES = (
    ((2 * R, 3 * R), BF),
    ((R, 6 * R), BF),
    ((6 * R, 2 * R), BF),
)


def load_outer(table_hbm, outer_ref, sem):
    return [
        pltpu.make_async_copy(table_hbm.at[0 : 2 * R, :], outer_ref.at[:, 0 : 2 * R], sem.at[0]),
        pltpu.make_async_copy(table_hbm.at[0 : 2 * R, 0:R], outer_ref.at[:, 2 * R : 3 * R], sem.at[1]),
    ]


def load_back(table_hbm, back_ref, sem):
    high, low = slice(2 * R, 3 * R), slice(3 * R, 4 * R)
    return [
        pltpu.make_async_copy(table_hbm.at[rows, :], back_ref.at[:, 2 * R * i : 2 * R * (i + 1)], sem.at[2 + i])
        for i, rows in enumerate((high, low, high))
    ]


def load_inner(table_hbm, inner_ref, sem):
    high, both = slice(4 * R, 6 * R), slice(4 * R, 8 * R)
    return [
        pltpu.make_async_copy(table_hbm.at[high, :], inner_ref.at[0 : 2 * R, :], sem.at[5]),
        pltpu.make_async_copy(table_hbm.at[both, :], inner_ref.at[2 * R : 6 * R, :], sem.at[6]),
    ]


def start(copies):
    for copy in copies:
        copy.start()
    return copies


def finish(copies):
    for copy in copies:
        copy.wait()


def split(value):
    high = value.astype(BF)
    return high, (value - high.astype(F32)).astype(BF)


def dot(left, right):
    return jnp.dot(left, right, preferred_element_type=F32)


CHUNK = 16


def chunks():
    return [slice(i, i + CHUNK) for i in range(0, R, CHUNK)]


def put_column(ref, where, rows, value):
    high, low = split(value)
    size = ref.shape[-2] // 3
    for place, part in enumerate((high, high, low)):
        ref[where, rows.start + place * size : rows.stop + place * size, :] = part


def put_row(ref, first, rows, left, right):
    rows = slice(first + rows.start, first + rows.stop)
    left_high, left_low = split(left)
    right_high, right_low = split(right)
    for place, part in enumerate((left_high, right_high, left_low, right_low, left_high, right_high)):
        ref[rows, place * R : (place + 1) * R] = part


def outer_stage(case, column_ref, first_ref, outer_ref, turn_ref, row_ref, base):
    first_ref[...] = dot(outer_ref[...], column_ref[case])
    for rows in chunks():
        real, imag = first_ref[rows, :], first_ref[R + rows.start : R + rows.stop, :]
        turn_real, turn_imag = turn_ref[0, rows, :], turn_ref[1, rows, :]
        put_row(
            row_ref, base, rows, real * turn_real - imag * turn_imag, real * turn_imag + imag * turn_real
        )


def taps_columns(taps_ref, column_ref):
    taps = jnp.concatenate([taps_ref[j] for j in range(3)], axis=0)
    padded = jnp.concatenate([taps, jnp.zeros((7, taps.shape[1]), F32)], axis=0)
    column_ref[:, 0:16] = padded.T


def gate_kernel(length_ref, taps_ref, features_ref, out_ref, column_ref, in_ref, send_ref, in_sem, out_sem):
    width = features_ref.shape[3]
    parts = in_ref.shape[0]
    group = in_ref.shape[2]
    copies = [
        pltpu.make_async_copy(
            features_ref.at[0, pl.ds(1, 2), pl.ds(group * part, group), :], in_ref.at[part], in_sem.at[part]
        )
        for part in range(parts)
    ]
    for copy in copies:
        copy.start()
    taps_columns(taps_ref, column_ref)
    limit = length_ref[0] - lax.axis_index("seq") * width
    lane = lax.broadcasted_iota(jnp.int32, (8, width), 1)
    near = lane[:, 0:128]
    valid = lane < limit
    sends = []
    for part in range(parts):
        copies[part].wait()
        for sub in range(group // 8):
            channel = part * group + sub * 8
            column = column_ref[channel : channel + 8, :]

            def stream(j):
                here = in_ref[part, j - 1, sub * 8 : sub * 8 + 8, :]
                one = pltpu.roll(here, 1, 1)
                two = pltpu.roll(here, 2, 1)
                t0, t1, t2 = (column[:, 3 * j + i : 3 * j + i + 1] for i in range(3))
                value = t0 * here + t1 * jnp.where(lane < 1, 0.0, one) + t2 * jnp.where(lane < 2, 0.0, two)
                over = t1 * jnp.where(near < 1, one[:, 0:128], 0.0) + t2 * jnp.where(
                    near < 2, two[:, 0:128], 0.0
                )
                return value, over

            key, key_over = stream(1)
            value, value_over = stream(2)
            gated = jnp.where(valid, key * value, 0.0)
            for tile in range(width // 128):
                row = channel * SPAN + (tile % 2) * 16 + tile // 2
                send_ref[pl.ds(row, 8, stride=SPAN), :] = gated[:, tile * 128 : tile * 128 + 128]
            flag = jnp.where(near < limit, 1.0, 0.0)
            edge = jnp.where(near < 2, key[:, 0:128], 0.0)
            for place, item in ((1, value[:, 0:128]), (2, key_over), (3, value_over), (4, flag)):
                inside = (near >= 2 * place) & (near < 2 * place + 2)
                edge = jnp.where(inside, pltpu.roll(item, 2 * place, 1), edge)
            send_ref[pl.ds(channel * SPAN + 32, 8, stride=SPAN), :] = edge
        rows = pl.ds(part * group * SPAN, group * SPAN)
        there = pl.ds(part * group * SPAN, group * SPAN)
        send = pltpu.make_async_copy(send_ref.at[rows, :], out_ref.at[there, :], out_sem.at[part])
        send.start()
        sends.append(send)
    for send in sends:
        send.wait()


def gate(lengths, short_filter, features):
    _, _, channels, width = features.shape
    parts = 4
    return pl.pallas_call(
        gate_kernel,
        in_specs=[SM, VM, HB],
        out_specs=HB,
        out_shape=jax.ShapeDtypeStruct((channels * SPAN, 128), F32),
        scratch_shapes=[
            pltpu.VMEM((channels, 128), F32),
            pltpu.VMEM((parts, 2, channels // parts, width), F32),
            pltpu.VMEM((channels * SPAN, 128), F32),
            pltpu.SemaphoreType.DMA((parts,)),
            pltpu.SemaphoreType.DMA((parts,)),
        ],
        compiler_params=pltpu.CompilerParams(vmem_limit_bytes=60 << 20),
        cost_estimate=pl.CostEstimate(flops=1 << 20, bytes_accessed=12 << 20, transcendentals=0),
        name="gate",
    )(lengths, short_filter, features)


def pair_kernel(mine_ref, other_ref, out_ref):
    x = lax.axis_index("x_lo")
    mine = jnp.where(x == 0, mine_ref[0:2, :], mine_ref[2:4, :])
    other = jnp.where(x == 0, other_ref[0:2, :], other_ref[2:4, :])
    parts = (jnp.where(x == 0, mine, other), jnp.where(x == 0, other, mine))
    for channel in range(2):
        for place in range(2):
            for row in range(32):
                out_ref[channel, place, row : row + 1, :] = parts[place][
                    channel : channel + 1, row * R : row * R + R
                ]


def pair_up(mine, other):
    return pl.pallas_call(
        pair_kernel,
        in_specs=[VM, VM],
        out_specs=VM,
        out_shape=jax.ShapeDtypeStruct((2, 2, 32, R), F32),
        compiler_params=pltpu.CompilerParams(vmem_limit_bytes=4 << 20),
        name="pair_up",
    )(mine, other)


def filter_kernel(
    skip_ref, p0, p1, p2, p3, table_hbm, turn_hbm, spec_ref, turn_ref, column_ref, first_ref, row_ref, outer_ref, inner_ref, sem
):
    outer_copies = start(load_outer(table_hbm, outer_ref, sem))
    turn_copies = start([pltpu.make_async_copy(turn_hbm, turn_ref, sem.at[7])])
    inner_copies = start(load_inner(table_hbm, inner_ref, sem))
    y, x = lax.axis_index("y"), lax.axis_index("x_lo")
    for away, part in enumerate((p0, p1, p2, p3)):
        first = lax.rem(y + 4 - away, 4) * 64
        for channel in range(2):
            for place in range(2):
                for half in range(2):
                    high, low = split(part[channel, place, 16 * half : 16 * half + 16, :])
                    for third, piece in enumerate((high, high, low)):
                        at = pl.multiple_of(third * R + first + 32 * place + 16 * half, 16)
                        column_ref[channel, pl.ds(at, 16), :] = piece
    finish(outer_copies + turn_copies)
    for channel in range(2):
        outer_stage(channel, column_ref, first_ref.at[channel], outer_ref, turn_ref, row_ref, channel * R)
    finish(inner_copies)
    spec = dot(row_ref[...], inner_ref[...]) * (1.0 / N)
    for channel in range(2):
        skip = skip_ref[2 * x + channel] * (1.0 / N)
        spec_ref[channel, 0] = spec[channel * R : (channel + 1) * R, 0:R] + skip
        spec_ref[channel, 1] = spec[channel * R : (channel + 1) * R, R : 2 * R]


def filter_spectrum(skip_gain, parts, table, turn):
    return pl.pallas_call(
        filter_kernel,
        in_specs=[SM] + [VM] * 4 + [HB] * 2,
        out_specs=[VM] * 2,
        out_shape=[jax.ShapeDtypeStruct((2, 2, R, R), F32), jax.ShapeDtypeStruct(turn.shape, F32)],
        scratch_shapes=[
            pltpu.VMEM((2, 3 * R, R), BF),
            pltpu.VMEM((2, 2 * R, R), F32),
            pltpu.VMEM((2 * R, 6 * R), BF),
            pltpu.VMEM(*TABLES[0]),
            pltpu.VMEM(*TABLES[2]),
            pltpu.SemaphoreType.DMA((8,)),
        ],
        compiler_params=pltpu.CompilerParams(vmem_limit_bytes=24 << 20),
        name="filter_spectrum",
    )(skip_gain, *parts, table, turn)


def conv_kernel(
    moved_ref,
    spec_ref,
    turn_ref,
    table_hbm,
    out_hbm,
    column_ref,
    first_ref,
    row_ref,
    mid_ref,
    last_ref,
    result_ref,
    outer_ref,
    back_ref,
    inner_ref,
    sem,
    out_sem,
):
    outer_copies = start(load_outer(table_hbm, outer_ref, sem))
    inner_copies = start(load_inner(table_hbm, inner_ref, sem))
    back_copies = start(load_back(table_hbm, back_ref, sem))
    blocks = N // 4096
    lane = lax.broadcasted_iota(jnp.int32, (blocks, 128), 1)
    block = lax.broadcasted_iota(jnp.int32, (blocks, 128), 0)
    for case in range(4):
        rep, channel = case // 2, case % 2
        begin = channel * SPAN
        edge = jnp.concatenate(
            [moved_ref[2 * b + rep, begin + 32 : begin + 33, :] for b in range(blocks)], axis=0
        )
        behind = jnp.where(block < 1, 0.0, pltpu.roll(edge, 1, 0))
        key = edge + pltpu.roll(behind, 124, 1)
        value = pltpu.roll(edge, 126, 1) + pltpu.roll(behind, 122, 1)
        mended = key * value * pltpu.roll(edge, 120, 1)
        for b in range(blocks):
            left = moved_ref[2 * b + rep, begin : begin + 16, :]
            right = moved_ref[2 * b + rep, begin + 16 : begin + 32, :]
            left = jnp.where((block < 1) & (lane < 2), mended[b : b + 1], left)
            put_column(column_ref, case, slice(16 * b, 16 * b + 16), jnp.concatenate([left, right], axis=1))
    finish(outer_copies)
    for case in range(4):
        outer_stage(case, column_ref, first_ref.at[case], outer_ref, turn_ref, row_ref, case * R)
    finish(inner_copies)
    sends = []
    size = GROUP * R
    for group in range(4 // GROUP):
        every = slice(group * size, (group + 1) * size)
        mid_ref[every, :] = dot(row_ref[every, :], inner_ref[...])
        for case in range(group * GROUP, (group + 1) * GROUP):
            channel = case % 2
            for rows in chunks():
                here = slice(case * R + rows.start, case * R + rows.stop)
                real, imag = mid_ref[here, 0:R], mid_ref[here, R : 2 * R]
                spec_real, spec_imag = spec_ref[channel, 0, rows, :], spec_ref[channel, 1, rows, :]
                put_row(
                    row_ref,
                    case * R,
                    rows,
                    real * spec_imag + imag * spec_real,
                    real * spec_real - imag * spec_imag,
                )
    for group in range(4 // GROUP):
        every = slice(group * size, (group + 1) * size)
        mid_ref[every, :] = dot(row_ref[every, :], inner_ref[...])
        if group == 0:
            finish(back_copies)
        for case in range(group * GROUP, (group + 1) * GROUP):
            rep, channel = case // 2, case % 2
            for rows in chunks():
                here = slice(case * R + rows.start, case * R + rows.stop)
                imag, real = mid_ref[here, 0:R], mid_ref[here, R : 2 * R]
                turn_real, turn_imag = turn_ref[0, rows, :], turn_ref[1, rows, :]
                put_column(last_ref, case, rows, real * turn_real + imag * turn_imag)
                below = slice(R + rows.start, R + rows.stop)
                put_column(last_ref, case, below, imag * turn_real - real * turn_imag)
            result = dot(back_ref[...], last_ref[case])
            for half in range(2):
                result_ref[case, :, half * 16 : half * 16 + 16, :] = result[
                    :, half * 128 : half * 128 + 128
                ].reshape(blocks, 16, 128)
            sends += start(
                [
                    pltpu.make_async_copy(
                        result_ref.at[case],
                        out_hbm.reshape(16, 2, 64, 128).at[:, rep, pl.ds(channel * 32, 32), :],
                        out_sem.at[case],
                    )
                ]
            )
    finish(sends)


GROUP = 2


def convolve(moved, spec, turn, table):
    return pl.pallas_call(
        conv_kernel,
        in_specs=[VM] * 3 + [HB],
        out_specs=HB,
        out_shape=jax.ShapeDtypeStruct((32, 64, 128), F32),
        scratch_shapes=[
            pltpu.VMEM((4, 3 * R, R), BF),
            pltpu.VMEM((4, 2 * R, R), F32),
            pltpu.VMEM((4 * R, 6 * R), BF),
            pltpu.VMEM((4 * R, 2 * R), F32),
            pltpu.VMEM((4, 6 * R, R), BF),
            pltpu.VMEM((4, 16, 32, 128), F32),
        ]
        + [pltpu.VMEM(*table_like) for table_like in TABLES]
        + [pltpu.SemaphoreType.DMA((8,)), pltpu.SemaphoreType.DMA((4,))],
        compiler_params=pltpu.CompilerParams(vmem_limit_bytes=60 << 20),
        name="convolve",
    )(moved, spec, turn, table)


def query_kernel(length_ref, taps_ref, tail_ref, features_ref, out_ref, column_ref):
    group, width = out_ref.shape

    @pl.when(pl.program_id(0) == 0)
    def _():
        taps_columns(taps_ref, column_ref)

    limit = length_ref[0] - lax.axis_index("seq") * width
    lane = lax.broadcasted_iota(jnp.int32, (8, width), 1)
    near = lane[:, 0:128]
    for sub in range(group // 8):
        rows = pl.ds(pl.multiple_of(pl.program_id(0) * group + sub * 8, 8), 8)
        column, tail = column_ref[rows, :], tail_ref[rows, :]
        here = features_ref[sub * 8 : sub * 8 + 8, :]
        t0, t1, t2 = (column[:, i : i + 1] for i in range(3))
        one = jnp.where(lane < 1, 0.0, pltpu.roll(here, 1, 1))
        two = jnp.where(lane < 2, 0.0, pltpu.roll(here, 2, 1))
        value = t0 * here + t1 * one + t2 * two
        out_ref[sub * 8 : sub * 8 + 8, :] = jnp.where(lane < limit, value, 0.0)
        far, last = tail[:, 126:127], tail[:, 127:128]
        mend = jnp.where(near == 0, t1 * last + t2 * far, jnp.where(near == 1, t2 * last, 0.0))
        out_ref[sub * 8 : sub * 8 + 8, 0:128] = jnp.where(near < limit, value[:, 0:128] + mend, 0.0)


def query(lengths, short_filter, tail, features):
    _, streams, channels, width = features.shape
    group = 16
    return pl.pallas_call(
        query_kernel,
        grid=(channels // group,),
        in_specs=[SM, VM, VM, pl.BlockSpec((None, None, group, width), lambda i: (0, 0, i, 0))],
        out_specs=pl.BlockSpec((group, width), lambda i: (i, 0)),
        out_shape=jax.ShapeDtypeStruct((channels, width), F32),
        scratch_shapes=[pltpu.VMEM((channels, 128), F32)],
        compiler_params=pltpu.CompilerParams(vmem_limit_bytes=12 << 20),
        name="query",
    )(lengths, short_filter, tail, features)


def mix_kernel(query_hbm, back_hbm, out_hbm, query_ref, back_ref, out_ref, sem):
    channels, width = out_ref.shape
    parts = 4
    group = channels // parts
    loads = []
    for part in range(parts):
        rows, there = pl.ds(group * part, group), pl.ds(32 * group * part, 32 * group)
        loads.append(
            start(
                [
                    pltpu.make_async_copy(query_hbm.at[rows, :], query_ref.at[rows, :], sem.at[0, part]),
                    pltpu.make_async_copy(back_hbm.at[there, :], back_ref.at[there, :], sem.at[1, part]),
                ]
            )
        )
    sends = []
    for part in range(parts):
        finish(loads[part])
        for sub in range(group // 8):
            channel = part * group + sub * 8
            for tile in range(width // 128):
                row = channel * 32 + (tile % 2) * 16 + tile // 2
                lanes = slice(tile * 128, tile * 128 + 128)
                out_ref[channel : channel + 8, lanes] = (
                    query_ref[channel : channel + 8, lanes] * back_ref[pl.ds(row, 8, stride=32), :]
                )
        rows = pl.ds(group * part, group)
        sends += start([pltpu.make_async_copy(out_ref.at[rows, :], out_hbm.at[0, rows, :], sem.at[2, part])])
    finish(sends)


def mix(query, returned):
    return pl.pallas_call(
        mix_kernel,
        in_specs=[HB, HB],
        out_specs=HB,
        out_shape=jax.ShapeDtypeStruct((1,) + query.shape, F32),
        scratch_shapes=[
            pltpu.VMEM(query.shape, F32),
            pltpu.VMEM(returned.shape, F32),
            pltpu.VMEM(query.shape, F32),
            pltpu.SemaphoreType.DMA((3, 4)),
        ],
        compiler_params=pltpu.CompilerParams(vmem_limit_bytes=60 << 20),
        name="mix",
    )(query, returned)


def exchange(blocks):
    return lax.all_to_all(blocks, ("seq", "x_lo"), split_axis=0, concat_axis=0, tiled=True)


def body(features, short_filter, long_filter, skip_gain, lengths):
    seq_dev = features.shape[3]
    n_seq = lax.axis_size("seq")
    table, turn = (jnp.asarray(t) for t in tables())
    other = lax.ppermute(long_filter, "x_lo", [(0, 1), (1, 0)])
    gated = gate(lengths, short_filter, features)
    gated, other = lax.optimization_barrier((gated, other))
    moved = exchange(gated.reshape(2 * n_seq, 2 * SPAN, 128))
    pair = pair_up(long_filter, other)
    parts = [pair] + [
        lax.ppermute(pair, "y", [(i, (i + away) % 4) for i in range(4)]) for away in range(1, 4)
    ]
    spec, turn = filter_spectrum(skip_gain, parts, table, turn)
    convolved = convolve(moved, spec, turn, table)
    returned = exchange(convolved)
    tail = lax.ppermute(features[0, 0, :, seq_dev - 128 :], "seq", [(i, i + 1) for i in range(n_seq - 1)])
    return mix(query(lengths, short_filter, tail, features), returned.reshape(2 * n_seq * 64, 128))


def solution(mesh):
    devices = mesh.devices
    reps, seqs = devices.shape
    finer = Mesh(devices.reshape(reps // 2, 2, seqs), ("y", "x_lo", "seq"))
    rep = ("y", "x_lo")
    return jax.shard_map(
        body,
        mesh=finer,
        in_specs=(P(rep, None, None, "seq"), P(), P("seq", rep), P("seq"), P(rep)),
        out_specs=P(rep, None, "seq"),
        check_vma=False,
    )
```

```python
import math

import jax
import jax.numpy as jnp
import ml_dtypes
import numpy as np
from jax import lax
from jax.experimental import pallas as pl
from jax.experimental.pallas import tpu as pltpu
from jax.sharding import Mesh
from jax.sharding import PartitionSpec as P

R = 256
N = R * R
BF = jnp.bfloat16
F32 = jnp.float32
SPAN = 36

VM = pl.BlockSpec(memory_space=pltpu.VMEM)
SM = pl.BlockSpec(memory_space=pltpu.SMEM)
HB = pl.BlockSpec(memory_space=pltpu.HBM)


def halves(table, axis):
    high = table.astype(np.float32).astype(ml_dtypes.bfloat16)
    low = (table - high.astype(np.float64)).astype(np.float32).astype(ml_dtypes.bfloat16)
    return np.concatenate([high, low], axis=axis)


def tables():
    row = np.arange(R, dtype=np.float64)
    first = 2.0 * math.pi / R * np.outer(row + 0.25, row)
    outer = np.concatenate([np.cos(first), -np.sin(first)], axis=0)
    twist = 2.0 * math.pi / N * np.outer(row + 0.25, row)
    turn = np.stack([np.cos(twist), -np.sin(twist)]).astype(np.float32)
    last = 2.0 * math.pi / R * np.outer(row, row)
    inner = np.block([[np.cos(last), -np.sin(last)], [np.sin(last), np.cos(last)]])
    return np.concatenate([halves(outer, 1), halves(outer.T, 0), halves(inner, 0)], axis=0), turn


TABLES = (
    ((2 * R, 3 * R), BF),
    ((R, 6 * R), BF),
    ((6 * R, 2 * R), BF),
)


def load_outer(table_hbm, outer_ref, sem):
    return [pltpu.make_async_copy(table_hbm.at[0 : 2 * R, :], outer_ref.at[:, 0 : 2 * R], sem)]


def load_back(table_hbm, back_ref, sem):
    return [
        pltpu.make_async_copy(
            table_hbm.at[(2 + i) * R : (3 + i) * R, :], back_ref.at[:, 2 * R * i : 2 * R * (i + 1)], sem.at[i]
        )
        for i in range(2)
    ]


def load_inner(table_hbm, inner_ref, sem):
    return [pltpu.make_async_copy(table_hbm.at[4 * R : 8 * R, :], inner_ref.at[2 * R : 6 * R, :], sem)]


def repeat_rows(ref, source, target, count):
    for i in range(0, count, 64):
        ref[target + i : target + i + 64, :] = ref[source + i : source + i + 64, :]


def repeat_lanes(ref, target, count):
    for i in range(0, ref.shape[0], 64):
        ref[i : i + 64, target : target + count] = ref[i : i + 64, 0:count]


def start(copies):
    for copy in copies:
        copy.start()
    return copies


def finish(copies):
    for copy in copies:
        copy.wait()


def split(value):
    high = value.astype(BF)
    return high, (value - high.astype(F32)).astype(BF)


def dot(left, right):
    return jnp.dot(left, right, preferred_element_type=F32)


CHUNK = 16


def chunks():
    return [slice(i, i + CHUNK) for i in range(0, R, CHUNK)]


def put_column(ref, case, rows, value):
    high, low = split(value)
    size = ref.shape[-2] // 3
    lanes = slice(case % 2 * R, (case % 2 + 1) * R)
    for place, part in enumerate((high, high, low)):
        ref[case // 2, rows.start + place * size : rows.stop + place * size, lanes] = part


def put_row(ref, first, rows, left, right):
    rows = slice(first + rows.start, first + rows.stop)
    left_high, left_low = split(left)
    right_high, right_low = split(right)
    for place, part in enumerate((left_high, right_high, left_low, right_low, left_high, right_high)):
        ref[rows, place * R : (place + 1) * R] = part


def outer_stage(pair, column_ref, first_ref, outer_ref, turn_ref, row_ref):
    first_ref[...] = dot(outer_ref[...], column_ref[pair])
    for side in range(2):
        lanes = slice(side * R, (side + 1) * R)
        for rows in chunks():
            real, imag = first_ref[rows, lanes], first_ref[R + rows.start : R + rows.stop, lanes]
            turn_real, turn_imag = turn_ref[0, rows, :], turn_ref[1, rows, :]
            put_row(
                row_ref,
                (2 * pair + side) * R,
                rows,
                real * turn_real - imag * turn_imag,
                real * turn_imag + imag * turn_real,
            )


def taps_columns(taps_ref, column_ref):
    taps = jnp.concatenate([taps_ref[j] for j in range(3)], axis=0)
    padded = jnp.concatenate([taps, jnp.zeros((7, taps.shape[1]), F32)], axis=0)
    column_ref[:, 0:16] = padded.T


def gate_kernel(length_ref, taps_hbm, features_ref, out_ref, taps_ref, column_ref, in_ref, send_ref, in_sem, out_sem):
    taps_copy = pltpu.make_async_copy(taps_hbm, taps_ref, in_sem.at[in_ref.shape[0]])
    taps_copy.start()
    width = features_ref.shape[3]
    parts = in_ref.shape[0]
    group = in_ref.shape[2]
    copies = [
        pltpu.make_async_copy(
            features_ref.at[0, pl.ds(1, 2), pl.ds(group * part, group), :], in_ref.at[part], in_sem.at[part]
        )
        for part in range(parts)
    ]
    for copy in copies:
        copy.start()
    taps_copy.wait()
    taps_columns(taps_ref, column_ref)
    limit = length_ref[...].reshape(1, 1) - lax.axis_index("seq") * width
    near = lax.broadcasted_iota(jnp.int32, (8, 128), 1)
    sends = []
    for part in range(parts):
        copies[part].wait()
        for sub in range(group // 8):
            channel = part * group + sub * 8
            column = column_ref[channel : channel + 8, :]

            tap = [[jnp.broadcast_to(column[:, 3 * j + i : 3 * j + i + 1], (8, 128)) for i in range(3)] for j in (1, 2)]

            def tile_of(j, tile):
                lanes = slice(tile * 128, tile * 128 + 128)
                return in_ref[part, j, sub * 8 : sub * 8 + 8, lanes]

            last = width // 128 - 1
            before = [tile_of(j, last) for j in range(2)]
            turned = [[pltpu.roll(before[j], i, 1) for i in (1, 2)] for j in range(2)]
            over = [
                tap[j][1] * jnp.where(near < 1, turned[j][0], 0.0) + tap[j][2] * jnp.where(near < 2, turned[j][1], 0.0)
                for j in range(2)
            ]
            turned = [[jnp.zeros((8, 128), F32)] * 2] * 2
            for tile in range(width // 128):
                values = []
                for j in range(2):
                    here = tile_of(j, tile)
                    one, two = pltpu.roll(here, 1, 1), pltpu.roll(here, 2, 1)
                    values.append(
                        tap[j][0] * here
                        + tap[j][1] * jnp.where(near < 1, turned[j][0], one)
                        + tap[j][2] * jnp.where(near < 2, turned[j][1], two)
                    )
                    turned = [turned[i] if i != j else [one, two] for i in range(2)]
                if tile == 0:
                    key, value = values
                row = channel * SPAN + (tile % 2) * 16 + tile // 2
                send_ref[pl.ds(row, 8, stride=SPAN), :] = jnp.where(
                    near + tile * 128 < limit, values[0] * values[1], 0.0
                )
            key_over, value_over = over
            flag = jnp.where(near < limit, 1.0, 0.0)
            edge = jnp.where(near < 2, key, 0.0)
            for place, item in ((1, value), (2, key_over), (3, value_over), (4, flag)):
                inside = (near >= 2 * place) & (near < 2 * place + 2)
                edge = jnp.where(inside, pltpu.roll(item, 2 * place, 1), edge)
            send_ref[pl.ds(channel * SPAN + 32, 8, stride=SPAN), :] = edge
        rows = pl.ds(part * group * SPAN, group * SPAN)
        there = pl.ds(part * group * SPAN, group * SPAN)
        send = pltpu.make_async_copy(send_ref.at[rows, :], out_ref.at[there, :], out_sem.at[part])
        send.start()
        sends.append(send)
    for send in sends:
        send.wait()


def gate(lengths, short_filter, features):
    _, _, channels, width = features.shape
    parts = 4
    return pl.pallas_call(
        gate_kernel,
        in_specs=[VM, HB, HB],
        out_specs=HB,
        out_shape=jax.ShapeDtypeStruct((channels * SPAN, 128), F32),
        scratch_shapes=[
            pltpu.VMEM(short_filter.shape, F32),
            pltpu.VMEM((channels, 128), F32),
            pltpu.VMEM((parts, 2, channels // parts, width), F32),
            pltpu.VMEM((channels * SPAN, 128), F32),
            pltpu.SemaphoreType.DMA((parts + 1,)),
            pltpu.SemaphoreType.DMA((parts,)),
        ],
        compiler_params=pltpu.CompilerParams(vmem_limit_bytes=60 << 20),
        cost_estimate=pl.CostEstimate(flops=1 << 20, bytes_accessed=12 << 20, transcendentals=0),
        name="gate",
    )(lengths, short_filter, features)


def pair_kernel(mine_ref, other_ref, out_ref):
    x = lax.axis_index("x_lo")
    mine = jnp.where(x == 0, mine_ref[0:2, :], mine_ref[2:4, :])
    other = jnp.where(x == 0, other_ref[0:2, :], other_ref[2:4, :])
    parts = (jnp.where(x == 0, mine, other), jnp.where(x == 0, other, mine))
    for channel in range(2):
        for place in range(2):
            for row in range(32):
                out_ref[channel, place, row : row + 1, :] = parts[place][
                    channel : channel + 1, row * R : row * R + R
                ]


def pair_up(mine, other):
    return pl.pallas_call(
        pair_kernel,
        in_specs=[VM, VM],
        out_specs=VM,
        out_shape=jax.ShapeDtypeStruct((2, 2, 32, R), F32),
        compiler_params=pltpu.CompilerParams(vmem_limit_bytes=4 << 20),
        name="pair_up",
    )(mine, other)


def filter_kernel(
    skip_ref,
    p0,
    p1,
    p2,
    p3,
    table_hbm,
    turn_hbm,
    spec_hbm,
    turn_ref,
    column_ref,
    first_ref,
    row_ref,
    spec_ref,
    outer_ref,
    inner_ref,
    sem,
):
    outer_copies = start(load_outer(table_hbm, outer_ref, sem.at[0]))
    turn_copies = start([pltpu.make_async_copy(turn_hbm, turn_ref, sem.at[1])])
    inner_copies = start(load_inner(table_hbm, inner_ref, sem.at[2]))
    y, x = lax.axis_index("y"), lax.axis_index("x_lo")
    for away, part in enumerate((p0, p1, p2, p3)):
        first = lax.rem(y + 4 - away, 4) * 64
        for channel in range(2):
            for place in range(2):
                for half in range(2):
                    high, low = split(part[channel, place, 16 * half : 16 * half + 16, :])
                    for third, piece in enumerate((high, high, low)):
                        at = pl.multiple_of(third * R + first + 32 * place + 16 * half, 16)
                        column_ref[0, pl.ds(at, 16), channel * R : (channel + 1) * R] = piece
    finish(outer_copies + turn_copies)
    repeat_lanes(outer_ref, 2 * R, R)
    outer_stage(0, column_ref, first_ref, outer_ref, turn_ref, row_ref)
    finish(inner_copies)
    repeat_rows(inner_ref, 2 * R, 0, 2 * R)
    sends = []
    for channel in range(2):
        spec = dot(row_ref[channel * R : (channel + 1) * R, :], inner_ref[...]) * (1.0 / N)
        spec_ref[channel, 0] = spec[:, 0:R] + skip_ref[2 * x + channel] * (1.0 / N)
        spec_ref[channel, 1] = spec[:, R : 2 * R]
        sends += start(
            [pltpu.make_async_copy(spec_ref.at[channel], spec_hbm.at[channel], sem.at[3 + channel])]
        )
    finish(sends)


def filter_spectrum(skip_gain, parts, table, turn):
    return pl.pallas_call(
        filter_kernel,
        in_specs=[SM] + [VM] * 4 + [HB] * 2,
        out_specs=HB,
        out_shape=jax.ShapeDtypeStruct((2, 2, R, R), F32),
        scratch_shapes=[
            pltpu.VMEM(turn.shape, F32),
            pltpu.VMEM((1, 3 * R, 2 * R), BF),
            pltpu.VMEM((2 * R, 2 * R), F32),
            pltpu.VMEM((2 * R, 6 * R), BF),
            pltpu.VMEM((2, 2, R, R), F32),
            pltpu.VMEM(*TABLES[0]),
            pltpu.VMEM(*TABLES[2]),
            pltpu.SemaphoreType.DMA((5,)),
        ],
        compiler_params=pltpu.CompilerParams(vmem_limit_bytes=40 << 20),
        name="filter_spectrum",
    )(skip_gain, *parts, table, turn)


def conv_kernel(
    moved_hbm,
    spec_hbm,
    turn_hbm,
    table_hbm,
    out_hbm,
    moved_ref,
    spec_ref,
    turn_ref,
    column_ref,
    first_ref,
    row_ref,
    mid_ref,
    last_ref,
    result_ref,
    outer_ref,
    back_ref,
    inner_ref,
    sem,
    out_sem,
):
    cut = 40
    moved_copies = [
        pltpu.make_async_copy(moved_hbm.at[:, rows, :], moved_ref.at[:, rows, :], sem.at[i])
        for i, rows in enumerate((slice(0, cut), slice(cut, 2 * SPAN)))
    ]
    start(moved_copies[0:1])
    outer_copies = start(load_outer(table_hbm, outer_ref, sem.at[2]))
    turn_copies = start([pltpu.make_async_copy(turn_hbm, turn_ref, sem.at[3])])
    start(moved_copies[1:2])
    inner_copies = start(load_inner(table_hbm, inner_ref, sem.at[4]))
    spec_copies = start([pltpu.make_async_copy(spec_hbm, spec_ref, sem.at[5])])
    back_copies = start(load_back(table_hbm, back_ref, sem.at[6:8]))
    blocks = N // 4096
    lane = lax.broadcasted_iota(jnp.int32, (blocks, 128), 1)
    block = lax.broadcasted_iota(jnp.int32, (blocks, 128), 0)
    for channel in range(2):
        finish(moved_copies[channel : channel + 1])
        begin = channel * SPAN
        for rep in range(2):
            case = 2 * channel + rep
            edge = jnp.concatenate(
                [moved_ref[2 * b + rep, begin + 32 : begin + 33, :] for b in range(blocks)], axis=0
            )
            behind = jnp.where(block < 1, 0.0, pltpu.roll(edge, 1, 0))
            key = edge + pltpu.roll(behind, 124, 1)
            value = pltpu.roll(edge, 126, 1) + pltpu.roll(behind, 122, 1)
            mended = key * value * pltpu.roll(edge, 120, 1)
            for b in range(blocks):
                left = moved_ref[2 * b + rep, begin : begin + 16, :]
                right = moved_ref[2 * b + rep, begin + 16 : begin + 32, :]
                left = jnp.where((block < 1) & (lane < 2), mended[b : b + 1], left)
                put_column(
                    column_ref, case, slice(16 * b, 16 * b + 16), jnp.concatenate([left, right], axis=1)
                )
        if channel == 0:
            finish(outer_copies + turn_copies)
            repeat_lanes(outer_ref, 2 * R, R)
        outer_stage(channel, column_ref, first_ref.at[channel], outer_ref, turn_ref, row_ref)
    finish(inner_copies + spec_copies + back_copies)
    repeat_rows(inner_ref, 2 * R, 0, 2 * R)
    repeat_lanes(back_ref, 4 * R, 2 * R)
    sends = []
    size = 2 * R
    def forward_inner(group):
        every = slice(group * size, (group + 1) * size)
        mid_ref[every, :] = dot(row_ref[every, :], inner_ref[...])

    def multiply(group):
        for case in range(2 * group, 2 * group + 2):
            channel = case // 2
            for rows in chunks():
                here = slice(case * R + rows.start, case * R + rows.stop)
                real, imag = mid_ref[here, 0:R], mid_ref[here, R : 2 * R]
                spec_real, spec_imag = spec_ref[channel, 0, rows, :], spec_ref[channel, 1, rows, :]
                put_row(
                    row_ref,
                    case * R,
                    rows,
                    real * spec_imag + imag * spec_real,
                    real * spec_real - imag * spec_imag,
                )

    def untwist(group):
        for case in range(2 * group, 2 * group + 2):
            for rows in chunks():
                here = slice(case * R + rows.start, case * R + rows.stop)
                imag, real = mid_ref[here, 0:R], mid_ref[here, R : 2 * R]
                turn_real, turn_imag = turn_ref[0, rows, :], turn_ref[1, rows, :]
                put_column(last_ref, case, rows, real * turn_real + imag * turn_imag)
                below = slice(R + rows.start, R + rows.stop)
                put_column(last_ref, case, below, imag * turn_real - real * turn_imag)

    def backward_outer(group):
        result = dot(back_ref[...], last_ref[group])
        for rep in range(2):
            for half in range(2):
                lanes = slice(rep * R + half * 128, rep * R + half * 128 + 128)
                result_ref[group, rep, :, half * 16 : half * 16 + 16, :] = result[:, lanes].reshape(
                    blocks, 16, 128
                )
            sends.extend(
                start(
                    [
                        pltpu.make_async_copy(
                            result_ref.at[group, rep],
                            out_hbm.reshape(16, 2, 64, 128).at[:, rep, pl.ds(group * 32, 32), :],
                            out_sem.at[2 * group + rep],
                        )
                    ]
                )
            )

    stages = (forward_inner, multiply, forward_inner, untwist, backward_outer)
    groups = 2
    for step in range(len(stages) + groups - 1):
        for group in range(groups):
            if 0 <= step - group < len(stages):
                stages[step - group](group)
    finish(sends)


def convolve(moved, spec, turn, table):
    return pl.pallas_call(
        conv_kernel,
        in_specs=[HB] * 4,
        out_specs=HB,
        out_shape=jax.ShapeDtypeStruct((32, 64, 128), F32),
        scratch_shapes=[
            pltpu.VMEM(moved.shape, F32),
            pltpu.VMEM(spec.shape, F32),
            pltpu.VMEM(turn.shape, F32),
            pltpu.VMEM((2, 3 * R, 2 * R), BF),
            pltpu.VMEM((2, 2 * R, 2 * R), F32),
            pltpu.VMEM((4 * R, 6 * R), BF),
            pltpu.VMEM((4 * R, 2 * R), F32),
            pltpu.VMEM((2, 6 * R, 2 * R), BF),
            pltpu.VMEM((2, 2, 16, 32, 128), F32),
        ]
        + [pltpu.VMEM(*table_like) for table_like in TABLES]
        + [pltpu.SemaphoreType.DMA((8,)), pltpu.SemaphoreType.DMA((4,))],
        compiler_params=pltpu.CompilerParams(vmem_limit_bytes=60 << 20),
        name="convolve",
    )(moved, spec, turn, table)


def query_kernel(length_hbm, taps_ref, tail_ref, features_ref, out_ref, length_ref, column_ref, sem):
    group, width = out_ref.shape

    @pl.when(pl.program_id(0) == 0)
    def _():
        finish(start([pltpu.make_async_copy(length_hbm, length_ref, sem)]))
        taps_columns(taps_ref, column_ref)

    limit = length_ref[0] - lax.axis_index("seq") * width
    lane = lax.broadcasted_iota(jnp.int32, (8, width), 1)
    near = lane[:, 0:128]
    for sub in range(group // 8):
        rows = pl.ds(pl.multiple_of(pl.program_id(0) * group + sub * 8, 8), 8)
        column, tail = column_ref[rows, :], tail_ref[rows, :]
        here = features_ref[sub * 8 : sub * 8 + 8, :]
        t0, t1, t2 = (column[:, i : i + 1] for i in range(3))
        one = jnp.where(lane < 1, 0.0, pltpu.roll(here, 1, 1))
        two = jnp.where(lane < 2, 0.0, pltpu.roll(here, 2, 1))
        value = t0 * here + t1 * one + t2 * two
        out_ref[sub * 8 : sub * 8 + 8, :] = jnp.where(lane < limit, value, 0.0)
        far, last = tail[:, 126:127], tail[:, 127:128]
        mend = jnp.where(near == 0, t1 * last + t2 * far, jnp.where(near == 1, t2 * last, 0.0))
        out_ref[sub * 8 : sub * 8 + 8, 0:128] = jnp.where(near < limit, value[:, 0:128] + mend, 0.0)


def query(lengths, short_filter, tail, features):
    _, streams, channels, width = features.shape
    group = 16
    return pl.pallas_call(
        query_kernel,
        grid=(channels // group,),
        in_specs=[HB, VM, VM, pl.BlockSpec((None, None, group, width), lambda i: (0, 0, i, 0))],
        out_specs=pl.BlockSpec((group, width), lambda i: (i, 0)),
        out_shape=jax.ShapeDtypeStruct((channels, width), F32),
        scratch_shapes=[
            pltpu.SMEM((1,), jnp.int32),
            pltpu.VMEM((channels, 128), F32),
            pltpu.SemaphoreType.DMA,
        ],
        compiler_params=pltpu.CompilerParams(vmem_limit_bytes=12 << 20),
        name="query",
    )(lengths, short_filter, tail, features)


def mix_kernel(query_hbm, back_hbm, out_hbm, query_ref, back_ref, out_ref, sem):
    channels, width = out_ref.shape
    parts = 4
    group = channels // parts
    loads = []
    for part in range(parts):
        rows, there = pl.ds(group * part, group), pl.ds(32 * group * part, 32 * group)
        loads.append(
            start(
                [
                    pltpu.make_async_copy(query_hbm.at[rows, :], query_ref.at[rows, :], sem.at[0, part]),
                    pltpu.make_async_copy(back_hbm.at[there, :], back_ref.at[there, :], sem.at[1, part]),
                ]
            )
        )
    sends = []
    for part in range(parts):
        finish(loads[part])
        for sub in range(group // 8):
            channel = part * group + sub * 8
            for tile in range(width // 128):
                row = channel * 32 + (tile % 2) * 16 + tile // 2
                lanes = slice(tile * 128, tile * 128 + 128)
                out_ref[channel : channel + 8, lanes] = (
                    query_ref[channel : channel + 8, lanes] * back_ref[pl.ds(row, 8, stride=32), :]
                )
        rows = pl.ds(group * part, group)
        sends += start([pltpu.make_async_copy(out_ref.at[rows, :], out_hbm.at[0, rows, :], sem.at[2, part])])
    finish(sends)


def mix(query, returned):
    return pl.pallas_call(
        mix_kernel,
        in_specs=[HB, HB],
        out_specs=HB,
        out_shape=jax.ShapeDtypeStruct((1,) + query.shape, F32),
        scratch_shapes=[
            pltpu.VMEM(query.shape, F32),
            pltpu.VMEM(returned.shape, F32),
            pltpu.VMEM(query.shape, F32),
            pltpu.SemaphoreType.DMA((3, 4)),
        ],
        compiler_params=pltpu.CompilerParams(vmem_limit_bytes=60 << 20),
        name="mix",
    )(query, returned)


def exchange(blocks):
    return lax.all_to_all(blocks, ("seq", "x_lo"), split_axis=0, concat_axis=0, tiled=True)


def body(features, short_filter, long_filter, skip_gain, lengths):
    seq_dev = features.shape[3]
    n_seq = lax.axis_size("seq")
    table, turn = (jnp.asarray(t) for t in tables())
    other = lax.ppermute(long_filter, "x_lo", [(0, 1), (1, 0)])
    gated = gate(lengths, short_filter, features)
    gated, other = lax.optimization_barrier((gated, other))
    moved = exchange(gated.reshape(2 * n_seq, 2 * SPAN, 128))
    pair = pair_up(long_filter, other)
    parts = [pair] + [
        lax.ppermute(pair, "y", [(i, (i + away) % 4) for i in range(4)]) for away in range(1, 4)
    ]
    spec = filter_spectrum(skip_gain, parts, table, turn)
    convolved = convolve(moved, spec, turn, table)
    returned = exchange(convolved)
    tail = lax.ppermute(features[0, 0, :, seq_dev - 128 :], "seq", [(i, i + 1) for i in range(n_seq - 1)])
    return mix(query(lengths, short_filter, tail, features), returned.reshape(2 * n_seq * 64, 128))


def solution(mesh):
    devices = mesh.devices
    reps, seqs = devices.shape
    finer = Mesh(devices.reshape(reps // 2, 2, seqs), ("y", "x_lo", "seq"))
    rep = ("y", "x_lo")
    return jax.shard_map(
        body,
        mesh=finer,
        in_specs=(P(rep, None, None, "seq"), P(), P("seq", rep), P("seq"), P(rep)),
        out_specs=P(rep, None, "seq"),
        check_vma=False,
    )
```

```python
import math

import jax
import jax.numpy as jnp
import ml_dtypes
import numpy as np
from jax import lax
from jax.experimental import pallas as pl
from jax.experimental.pallas import tpu as pltpu
from jax.sharding import Mesh
from jax.sharding import PartitionSpec as P

R = 256
N = R * R
BF = jnp.bfloat16
F32 = jnp.float32
SPAN = 36

VM = pl.BlockSpec(memory_space=pltpu.VMEM)
SM = pl.BlockSpec(memory_space=pltpu.SMEM)
HB = pl.BlockSpec(memory_space=pltpu.HBM)


def halves(table, axis):
    high = table.astype(np.float32).astype(ml_dtypes.bfloat16)
    low = (table - high.astype(np.float64)).astype(np.float32).astype(ml_dtypes.bfloat16)
    return np.concatenate([high, low], axis=axis)


def tables():
    row = np.arange(R, dtype=np.float64)
    first = 2.0 * math.pi / R * np.outer(row + 0.25, row)
    outer = np.concatenate([np.cos(first), -np.sin(first)], axis=0)
    twist = 2.0 * math.pi / N * np.outer(row + 0.25, row)
    turn = np.stack([np.cos(twist), -np.sin(twist)]).astype(np.float32)
    last = 2.0 * math.pi / R * np.outer(row, row)
    inner = np.block([[np.cos(last), -np.sin(last)], [np.sin(last), np.cos(last)]])
    return np.concatenate([halves(outer, 1), halves(outer.T, 0), halves(inner, 0)], axis=0), turn


TABLES = (
    ((2 * R, 3 * R), BF),
    ((R, 6 * R), BF),
    ((6 * R, 2 * R), BF),
)


def load_outer(table_hbm, outer_ref, sem):
    return [pltpu.make_async_copy(table_hbm.at[0 : 2 * R, :], outer_ref.at[:, 0 : 2 * R], sem)]


def load_back(table_hbm, back_ref, sem):
    return [
        pltpu.make_async_copy(
            table_hbm.at[(2 + i) * R : (3 + i) * R, :], back_ref.at[:, 2 * R * i : 2 * R * (i + 1)], sem.at[i]
        )
        for i in range(2)
    ]


def load_inner(table_hbm, inner_ref, sem):
    return [pltpu.make_async_copy(table_hbm.at[4 * R : 8 * R, :], inner_ref.at[2 * R : 6 * R, :], sem)]


def repeat_rows(ref, source, target, count):
    for i in range(0, count, 64):
        ref[target + i : target + i + 64, :] = ref[source + i : source + i + 64, :]


def repeat_lanes(ref, target, count):
    for i in range(0, ref.shape[0], 64):
        ref[i : i + 64, target : target + count] = ref[i : i + 64, 0:count]


def start(copies):
    for copy in copies:
        copy.start()
    return copies


def finish(copies):
    for copy in copies:
        copy.wait()


def split(value):
    high = value.astype(BF)
    return high, (value - high.astype(F32)).astype(BF)


def dot(left, right):
    return jnp.dot(left, right, preferred_element_type=F32)


CHUNK = 16


def chunks():
    return [slice(i, i + CHUNK) for i in range(0, R, CHUNK)]


def put_column(ref, case, rows, value):
    high, low = split(value)
    size = ref.shape[-2] // 3
    lanes = slice(case % 2 * R, (case % 2 + 1) * R)
    for place, part in enumerate((high, high, low)):
        ref[case // 2, rows.start + place * size : rows.stop + place * size, lanes] = part


def put_row(ref, first, rows, left, right):
    rows = slice(first + rows.start, first + rows.stop)
    left_high, left_low = split(left)
    right_high, right_low = split(right)
    for place, part in enumerate((left_high, right_high, left_low, right_low, left_high, right_high)):
        ref[rows, place * R : (place + 1) * R] = part


def outer_stage(pair, column_ref, first_ref, outer_ref, turn_ref, row_ref):
    first_ref[...] = dot(outer_ref[...], column_ref[pair])
    for side in range(2):
        lanes = slice(side * R, (side + 1) * R)
        for rows in chunks():
            real, imag = first_ref[rows, lanes], first_ref[R + rows.start : R + rows.stop, lanes]
            turn_real, turn_imag = turn_ref[0, rows, :], turn_ref[1, rows, :]
            put_row(
                row_ref,
                (2 * pair + side) * R,
                rows,
                real * turn_real - imag * turn_imag,
                real * turn_imag + imag * turn_real,
            )


def taps_columns(taps_ref, column_ref):
    taps = jnp.concatenate([taps_ref[j] for j in range(3)], axis=0)
    padded = jnp.concatenate([taps, jnp.zeros((7, taps.shape[1]), F32)], axis=0)
    column_ref[:, 0:16] = padded.T


def gate_kernel(length_ref, taps_hbm, features_ref, out_ref, taps_ref, column_ref, in_ref, send_ref, in_sem, out_sem):
    taps_copy = pltpu.make_async_copy(taps_hbm, taps_ref, in_sem.at[in_ref.shape[0]])
    taps_copy.start()
    width = features_ref.shape[3]
    parts = in_ref.shape[0]
    group = in_ref.shape[2]
    copies = [
        pltpu.make_async_copy(
            features_ref.at[0, pl.ds(1, 2), pl.ds(group * part, group), :], in_ref.at[part], in_sem.at[part]
        )
        for part in range(parts)
    ]
    for copy in copies:
        copy.start()
    taps_copy.wait()
    taps_columns(taps_ref, column_ref)
    limit = length_ref[...].reshape(1, 1) - lax.axis_index("seq") * width
    near = lax.broadcasted_iota(jnp.int32, (8, 128), 1)
    sends = []
    for part in range(parts):
        copies[part].wait()
        for sub in range(group // 8):
            channel = part * group + sub * 8
            column = column_ref[channel : channel + 8, :]

            tap = [[jnp.broadcast_to(column[:, 3 * j + i : 3 * j + i + 1], (8, 128)) for i in range(3)] for j in (1, 2)]

            def tile_of(j, tile):
                lanes = slice(tile * 128, tile * 128 + 128)
                return in_ref[part, j, sub * 8 : sub * 8 + 8, lanes]

            last = width // 128 - 1
            before = [tile_of(j, last) for j in range(2)]
            turned = [[pltpu.roll(before[j], i, 1) for i in (1, 2)] for j in range(2)]
            over = [
                tap[j][1] * jnp.where(near < 1, turned[j][0], 0.0) + tap[j][2] * jnp.where(near < 2, turned[j][1], 0.0)
                for j in range(2)
            ]
            turned = [[jnp.zeros((8, 128), F32)] * 2] * 2
            for tile in range(width // 128):
                values = []
                for j in range(2):
                    here = tile_of(j, tile)
                    one, two = pltpu.roll(here, 1, 1), pltpu.roll(here, 2, 1)
                    values.append(
                        tap[j][0] * here
                        + tap[j][1] * jnp.where(near < 1, turned[j][0], one)
                        + tap[j][2] * jnp.where(near < 2, turned[j][1], two)
                    )
                    turned = [turned[i] if i != j else [one, two] for i in range(2)]
                if tile == 0:
                    key, value = values
                row = channel * SPAN + (tile % 2) * 16 + tile // 2
                send_ref[pl.ds(row, 8, stride=SPAN), :] = jnp.where(
                    near + tile * 128 < limit, values[0] * values[1], 0.0
                )
            key_over, value_over = over
            flag = jnp.where(near < limit, 1.0, 0.0)
            edge = jnp.where(near < 2, key, 0.0)
            for place, item in ((1, value), (2, key_over), (3, value_over), (4, flag)):
                inside = (near >= 2 * place) & (near < 2 * place + 2)
                edge = jnp.where(inside, pltpu.roll(item, 2 * place, 1), edge)
            send_ref[pl.ds(channel * SPAN + 32, 8, stride=SPAN), :] = edge
        rows = pl.ds(part * group * SPAN, group * SPAN)
        there = pl.ds(part * group * SPAN, group * SPAN)
        send = pltpu.make_async_copy(send_ref.at[rows, :], out_ref.at[there, :], out_sem.at[part])
        send.start()
        sends.append(send)
    for send in sends:
        send.wait()


def gate(lengths, short_filter, features):
    _, _, channels, width = features.shape
    parts = 4
    return pl.pallas_call(
        gate_kernel,
        in_specs=[VM, HB, HB],
        out_specs=HB,
        out_shape=jax.ShapeDtypeStruct((channels * SPAN, 128), F32),
        scratch_shapes=[
            pltpu.VMEM(short_filter.shape, F32),
            pltpu.VMEM((channels, 128), F32),
            pltpu.VMEM((parts, 2, channels // parts, width), F32),
            pltpu.VMEM((channels * SPAN, 128), F32),
            pltpu.SemaphoreType.DMA((parts + 1,)),
            pltpu.SemaphoreType.DMA((parts,)),
        ],
        compiler_params=pltpu.CompilerParams(vmem_limit_bytes=60 << 20),
        cost_estimate=pl.CostEstimate(flops=1 << 20, bytes_accessed=12 << 20, transcendentals=0),
        name="gate",
    )(lengths, short_filter, features)


def pair_kernel(mine_ref, other_ref, out_ref):
    x = lax.axis_index("x_lo")
    mine = jnp.where(x == 0, mine_ref[0:2, :], mine_ref[2:4, :])
    other = jnp.where(x == 0, other_ref[0:2, :], other_ref[2:4, :])
    parts = (jnp.where(x == 0, mine, other), jnp.where(x == 0, other, mine))
    for channel in range(2):
        for place in range(2):
            for row in range(32):
                out_ref[channel, place, row : row + 1, :] = parts[place][
                    channel : channel + 1, row * R : row * R + R
                ]


def pair_up(mine, other):
    return pl.pallas_call(
        pair_kernel,
        in_specs=[VM, VM],
        out_specs=VM,
        out_shape=jax.ShapeDtypeStruct((2, 2, 32, R), F32),
        compiler_params=pltpu.CompilerParams(vmem_limit_bytes=4 << 20),
        name="pair_up",
    )(mine, other)


def filter_kernel(
    skip_ref,
    p0,
    p1,
    p2,
    p3,
    table_hbm,
    turn_hbm,
    spec_hbm,
    turn_ref,
    column_ref,
    first_ref,
    row_ref,
    spec_ref,
    outer_ref,
    inner_ref,
    sem,
):
    outer_copies = start(load_outer(table_hbm, outer_ref, sem.at[0]))
    turn_copies = start([pltpu.make_async_copy(turn_hbm, turn_ref, sem.at[1])])
    inner_copies = start(load_inner(table_hbm, inner_ref, sem.at[2]))
    y, x = lax.axis_index("y"), lax.axis_index("x_lo")
    for away, part in enumerate((p0, p1, p2, p3)):
        first = lax.rem(y + 4 - away, 4) * 64
        for channel in range(2):
            for place in range(2):
                for half in range(2):
                    high, low = split(part[channel, place, 16 * half : 16 * half + 16, :])
                    for third, piece in enumerate((high, high, low)):
                        at = pl.multiple_of(third * R + first + 32 * place + 16 * half, 16)
                        column_ref[0, pl.ds(at, 16), channel * R : (channel + 1) * R] = piece
    finish(outer_copies + turn_copies)
    repeat_lanes(outer_ref, 2 * R, R)
    outer_stage(0, column_ref, first_ref, outer_ref, turn_ref, row_ref)
    finish(inner_copies)
    repeat_rows(inner_ref, 2 * R, 0, 2 * R)
    sends = []
    for channel in range(2):
        spec = dot(row_ref[channel * R : (channel + 1) * R, :], inner_ref[...]) * (1.0 / N)
        spec_ref[channel, 0] = spec[:, 0:R] + skip_ref[2 * x + channel] * (1.0 / N)
        spec_ref[channel, 1] = spec[:, R : 2 * R]
        sends += start(
            [pltpu.make_async_copy(spec_ref.at[channel], spec_hbm.at[channel], sem.at[3 + channel])]
        )
    finish(sends)


def filter_spectrum(skip_gain, parts, table, turn):
    return pl.pallas_call(
        filter_kernel,
        in_specs=[SM] + [VM] * 4 + [HB] * 2,
        out_specs=HB,
        out_shape=jax.ShapeDtypeStruct((2, 2, R, R), F32),
        scratch_shapes=[
            pltpu.VMEM(turn.shape, F32),
            pltpu.VMEM((1, 3 * R, 2 * R), BF),
            pltpu.VMEM((2 * R, 2 * R), F32),
            pltpu.VMEM((2 * R, 6 * R), BF),
            pltpu.VMEM((2, 2, R, R), F32),
            pltpu.VMEM(*TABLES[0]),
            pltpu.VMEM(*TABLES[2]),
            pltpu.SemaphoreType.DMA((5,)),
        ],
        compiler_params=pltpu.CompilerParams(vmem_limit_bytes=40 << 20),
        name="filter_spectrum",
    )(skip_gain, *parts, table, turn)


def conv_kernel(
    moved_hbm,
    spec_hbm,
    turn_hbm,
    table_hbm,
    out_hbm,
    moved_ref,
    spec_ref,
    turn_ref,
    column_ref,
    first_ref,
    row_ref,
    mid_ref,
    last_ref,
    result_ref,
    outer_ref,
    back_ref,
    inner_ref,
    sem,
    out_sem,
):
    cut = 40
    moved_copies = [
        pltpu.make_async_copy(moved_hbm.at[:, rows, :], moved_ref.at[:, rows, :], sem.at[i])
        for i, rows in enumerate((slice(0, cut), slice(cut, 2 * SPAN)))
    ]
    start(moved_copies[0:1])
    outer_copies = start(load_outer(table_hbm, outer_ref, sem.at[2]))
    turn_copies = start([pltpu.make_async_copy(turn_hbm, turn_ref, sem.at[3])])
    start(moved_copies[1:2])
    inner_copies = start(load_inner(table_hbm, inner_ref, sem.at[4]))
    spec_copies = start([pltpu.make_async_copy(spec_hbm, spec_ref, sem.at[5])])
    back_copies = start(load_back(table_hbm, back_ref, sem.at[6:8]))
    blocks = N // 4096
    lane = lax.broadcasted_iota(jnp.int32, (blocks, 128), 1)
    block = lax.broadcasted_iota(jnp.int32, (blocks, 128), 0)
    for channel in range(2):
        finish(moved_copies[channel : channel + 1])
        begin = channel * SPAN
        for rep in range(2):
            case = 2 * channel + rep
            edge = jnp.concatenate(
                [moved_ref[2 * b + rep, begin + 32 : begin + 33, :] for b in range(blocks)], axis=0
            )
            behind = jnp.where(block < 1, 0.0, pltpu.roll(edge, 1, 0))
            key = edge + pltpu.roll(behind, 124, 1)
            value = pltpu.roll(edge, 126, 1) + pltpu.roll(behind, 122, 1)
            mended = key * value * pltpu.roll(edge, 120, 1)
            for b in range(blocks):
                left = moved_ref[2 * b + rep, begin : begin + 16, :]
                right = moved_ref[2 * b + rep, begin + 16 : begin + 32, :]
                left = jnp.where((block < 1) & (lane < 2), mended[b : b + 1], left)
                put_column(
                    column_ref, case, slice(16 * b, 16 * b + 16), jnp.concatenate([left, right], axis=1)
                )
        if channel == 0:
            finish(outer_copies + turn_copies)
            repeat_lanes(outer_ref, 2 * R, R)
        outer_stage(channel, column_ref, first_ref.at[channel], outer_ref, turn_ref, row_ref)
    finish(inner_copies + spec_copies + back_copies)
    repeat_rows(inner_ref, 2 * R, 0, 2 * R)
    repeat_lanes(back_ref, 4 * R, 2 * R)
    sends = []
    size = 2 * R
    def forward_inner(group):
        every = slice(group * size, (group + 1) * size)
        mid_ref[every, :] = dot(row_ref[every, :], inner_ref[...])

    def multiply(group):
        for case in range(2 * group, 2 * group + 2):
            channel = case // 2
            for rows in chunks():
                here = slice(case * R + rows.start, case * R + rows.stop)
                real, imag = mid_ref[here, 0:R], mid_ref[here, R : 2 * R]
                spec_real, spec_imag = spec_ref[channel, 0, rows, :], spec_ref[channel, 1, rows, :]
                put_row(
                    row_ref,
                    case * R,
                    rows,
                    real * spec_imag + imag * spec_real,
                    real * spec_real - imag * spec_imag,
                )

    def untwist(group):
        for case in range(2 * group, 2 * group + 2):
            for rows in chunks():
                here = slice(case * R + rows.start, case * R + rows.stop)
                imag, real = mid_ref[here, 0:R], mid_ref[here, R : 2 * R]
                turn_real, turn_imag = turn_ref[0, rows, :], turn_ref[1, rows, :]
                put_column(last_ref, case, rows, real * turn_real + imag * turn_imag)
                below = slice(R + rows.start, R + rows.stop)
                put_column(last_ref, case, below, imag * turn_real - real * turn_imag)

    def backward_outer(group):
        result = dot(back_ref[...], last_ref[group])
        for rep in range(2):
            for half in range(2):
                lanes = slice(rep * R + half * 128, rep * R + half * 128 + 128)
                result_ref[group, rep, :, half * 16 : half * 16 + 16, :] = result[:, lanes].reshape(
                    blocks, 16, 128
                )
            sends.extend(
                start(
                    [
                        pltpu.make_async_copy(
                            result_ref.at[group, rep],
                            out_hbm.reshape(16, 2, 64, 128).at[:, rep, pl.ds(group * 32, 32), :],
                            out_sem.at[2 * group + rep],
                        )
                    ]
                )
            )

    stages = (forward_inner, multiply, forward_inner, untwist, backward_outer)
    groups = 2
    for step in range(len(stages) + groups - 1):
        for group in range(groups):
            if 0 <= step - group < len(stages):
                stages[step - group](group)
    finish(sends)


def convolve(moved, spec, turn, table):
    return pl.pallas_call(
        conv_kernel,
        in_specs=[HB] * 4,
        out_specs=HB,
        out_shape=jax.ShapeDtypeStruct((32, 64, 128), F32),
        scratch_shapes=[
            pltpu.VMEM(moved.shape, F32),
            pltpu.VMEM(spec.shape, F32),
            pltpu.VMEM(turn.shape, F32),
            pltpu.VMEM((2, 3 * R, 2 * R), BF),
            pltpu.VMEM((2, 2 * R, 2 * R), F32),
            pltpu.VMEM((4 * R, 6 * R), BF),
            pltpu.VMEM((4 * R, 2 * R), F32),
            pltpu.VMEM((2, 6 * R, 2 * R), BF),
            pltpu.VMEM((2, 2, 16, 32, 128), F32),
        ]
        + [pltpu.VMEM(*table_like) for table_like in TABLES]
        + [pltpu.SemaphoreType.DMA((8,)), pltpu.SemaphoreType.DMA((4,))],
        compiler_params=pltpu.CompilerParams(vmem_limit_bytes=60 << 20),
        name="convolve",
    )(moved, spec, turn, table)


def query_kernel(length_hbm, taps_ref, features_ref, out_ref, edge_ref, length_ref, column_ref, sem):
    group, width = out_ref.shape

    @pl.when(pl.program_id(0) == 0)
    def _():
        finish(start([pltpu.make_async_copy(length_hbm, length_ref, sem)]))
        taps_columns(taps_ref, column_ref)

    limit = length_ref[0] - lax.axis_index("seq") * width
    lane = lax.broadcasted_iota(jnp.int32, (8, width), 1)
    near = lane[:, 0:128]
    for sub in range(group // 8):
        rows = pl.ds(pl.multiple_of(pl.program_id(0) * group + sub * 8, 8), 8)
        column = column_ref[rows, :]
        here = features_ref[sub * 8 : sub * 8 + 8, :]
        t0, t1, t2 = (column[:, i : i + 1] for i in range(3))
        one = jnp.where(lane < 1, 0.0, pltpu.roll(here, 1, 1))
        two = jnp.where(lane < 2, 0.0, pltpu.roll(here, 2, 1))
        value = t0 * here + t1 * one + t2 * two
        out_ref[sub * 8 : sub * 8 + 8, :] = jnp.where(lane < limit, value, 0.0)
        here = slice(sub * 8, sub * 8 + 8)
        edge_ref[here, 0:128] = jnp.where((near < 1) & (near < limit), t1, 0.0)
        edge_ref[here, 128:256] = jnp.where((near < 2) & (near < limit), t2, 0.0)


def query(lengths, short_filter, features):
    _, streams, channels, width = features.shape
    group = 16
    return pl.pallas_call(
        query_kernel,
        grid=(channels // group,),
        in_specs=[HB, VM, pl.BlockSpec((None, None, group, width), lambda i: (0, 0, i, 0))],
        out_specs=[
            pl.BlockSpec((group, width), lambda i: (i, 0)),
            pl.BlockSpec((group, 256), lambda i: (i, 0)),
        ],
        out_shape=[
            jax.ShapeDtypeStruct((channels, width), F32),
            jax.ShapeDtypeStruct((channels, 256), F32),
        ],
        scratch_shapes=[
            pltpu.SMEM((1,), jnp.int32),
            pltpu.VMEM((channels, 128), F32),
            pltpu.SemaphoreType.DMA,
        ],
        compiler_params=pltpu.CompilerParams(vmem_limit_bytes=12 << 20),
        name="query",
    )(lengths, short_filter, features)


def mix_kernel(
    query_hbm, edge_hbm, tail_hbm, back_hbm, out_hbm, query_ref, edge_ref, tail_ref, back_ref, out_ref, sem
):
    channels, width = out_ref.shape
    parts = 4
    group = channels // parts
    small = start(
        [
            pltpu.make_async_copy(edge_hbm, edge_ref, sem.at[3, 0]),
            pltpu.make_async_copy(tail_hbm, tail_ref, sem.at[3, 1]),
        ]
    )
    loads = []
    for part in range(parts):
        rows, there = pl.ds(group * part, group), pl.ds(32 * group * part, 32 * group)
        loads.append(
            start(
                [
                    pltpu.make_async_copy(query_hbm.at[rows, :], query_ref.at[rows, :], sem.at[0, part]),
                    pltpu.make_async_copy(back_hbm.at[there, :], back_ref.at[there, :], sem.at[1, part]),
                ]
            )
        )
    finish(small)
    sends = []
    for part in range(parts):
        finish(loads[part])
        for sub in range(group // 8):
            channel = part * group + sub * 8
            here = slice(channel, channel + 8)
            tail = tail_ref[here, :]
            mend = pltpu.roll(tail, 1, 1) * edge_ref[here, 0:128] + pltpu.roll(tail, 2, 1) * edge_ref[here, 128:256]
            for tile in range(width // 128):
                row = channel * 32 + (tile % 2) * 16 + tile // 2
                lanes = slice(tile * 128, tile * 128 + 128)
                value = query_ref[here, lanes]
                if tile == 0:
                    value = value + mend
                out_ref[here, lanes] = value * back_ref[pl.ds(row, 8, stride=32), :]
        rows = pl.ds(group * part, group)
        sends += start([pltpu.make_async_copy(out_ref.at[rows, :], out_hbm.at[0, rows, :], sem.at[2, part])])
    finish(sends)


def mix(query, edge, tail, returned):
    return pl.pallas_call(
        mix_kernel,
        in_specs=[HB] * 4,
        out_specs=HB,
        out_shape=jax.ShapeDtypeStruct((1,) + query.shape, F32),
        scratch_shapes=[
            pltpu.VMEM(query.shape, F32),
            pltpu.VMEM(edge.shape, F32),
            pltpu.VMEM(tail.shape, F32),
            pltpu.VMEM(returned.shape, F32),
            pltpu.VMEM(query.shape, F32),
            pltpu.SemaphoreType.DMA((4, 4)),
        ],
        compiler_params=pltpu.CompilerParams(vmem_limit_bytes=60 << 20),
        name="mix",
    )(query, edge, tail, returned)


def exchange(blocks):
    return lax.all_to_all(blocks, ("seq", "x_lo"), split_axis=0, concat_axis=0, tiled=True)


def body(features, short_filter, long_filter, skip_gain, lengths):
    seq_dev = features.shape[3]
    n_seq = lax.axis_size("seq")
    table, turn = (jnp.asarray(t) for t in tables())
    other = lax.ppermute(long_filter, "x_lo", [(0, 1), (1, 0)])
    gated = gate(lengths, short_filter, features)
    gated, other = lax.optimization_barrier((gated, other))
    moved = exchange(gated.reshape(2 * n_seq, 2 * SPAN, 128))
    pair = pair_up(long_filter, other)
    parts = [pair] + [
        lax.ppermute(pair, "y", [(i, (i + away) % 4) for i in range(4)]) for away in range(1, 4)
    ]
    spec = filter_spectrum(skip_gain, parts, table, turn)
    convolved = convolve(moved, spec, turn, table)
    returned = exchange(convolved)
    tail = lax.ppermute(features[0, 0, :, seq_dev - 128 :], "seq", [(i, i + 1) for i in range(n_seq - 1)])
    gates, edge = query(lengths, short_filter, features)
    return mix(gates, edge, tail, returned.reshape(2 * n_seq * 64, 128))


def solution(mesh):
    devices = mesh.devices
    reps, seqs = devices.shape
    finer = Mesh(devices.reshape(reps // 2, 2, seqs), ("y", "x_lo", "seq"))
    rep = ("y", "x_lo")
    return jax.shard_map(
        body,
        mesh=finer,
        in_specs=(P(rep, None, None, "seq"), P(), P("seq", rep), P("seq"), P(rep)),
        out_specs=P(rep, None, "seq"),
        check_vma=False,
    )
```

```python
import math

import jax
import jax.numpy as jnp
import ml_dtypes
import numpy as np
from jax import lax
from jax.experimental import pallas as pl
from jax.experimental.pallas import tpu as pltpu
from jax.sharding import Mesh
from jax.sharding import PartitionSpec as P

R = 256
N = R * R
BF = jnp.bfloat16
F32 = jnp.float32
SPAN = 36

VM = pl.BlockSpec(memory_space=pltpu.VMEM)
SM = pl.BlockSpec(memory_space=pltpu.SMEM)
HB = pl.BlockSpec(memory_space=pltpu.HBM)


def halves(table, axis):
    high = table.astype(np.float32).astype(ml_dtypes.bfloat16)
    low = (table - high.astype(np.float64)).astype(np.float32).astype(ml_dtypes.bfloat16)
    return np.concatenate([high, low], axis=axis)


def tables():
    row = np.arange(R, dtype=np.float64)
    first = 2.0 * math.pi / R * np.outer(row + 0.25, row)
    outer = np.concatenate([np.cos(first), -np.sin(first)], axis=0)
    twist = 2.0 * math.pi / N * np.outer(row + 0.25, row)
    turn = np.stack([np.cos(twist), -np.sin(twist)]).astype(np.float32)
    last = 2.0 * math.pi / R * np.outer(row, row)
    cos, sin = np.cos(last), -np.sin(last)
    inner = np.concatenate([cos, sin - cos, -cos - sin], axis=0)
    return np.concatenate([halves(outer, 1), halves(outer.T, 0), halves(inner, 1)], axis=0), turn


TABLES = (
    ((2 * R, 3 * R), BF),
    ((R, 6 * R), BF),
    ((3, 3 * R, R), BF),
)


def load_outer(table_hbm, outer_ref, sem):
    return [pltpu.make_async_copy(table_hbm.at[0 : 2 * R, :], outer_ref.at[:, 0 : 2 * R], sem)]


def load_back(table_hbm, back_ref, sem):
    return [
        pltpu.make_async_copy(
            table_hbm.at[(2 + i) * R : (3 + i) * R, :], back_ref.at[:, 2 * R * i : 2 * R * (i + 1)], sem.at[i]
        )
        for i in range(2)
    ]


def load_inner(table_hbm, inner_ref, sem):
    stack = table_hbm.reshape(7, R, 2 * R)
    return [
        pltpu.make_async_copy(
            stack.at[4:7, :, i * R : (i + 1) * R], inner_ref.at[:, (i + 1) * R : (i + 2) * R, :], sem.at[i]
        )
        for i in range(2)
    ]


def repeat_inner(ref):
    for third in range(3):
        for i in range(0, R, 64):
            ref[third, i : i + 64, :] = ref[third, R + i : R + i + 64, :]


def repeat_lanes(ref, target, count):
    for i in range(0, ref.shape[0], 64):
        ref[i : i + 64, target : target + count] = ref[i : i + 64, 0:count]


def start(copies):
    for copy in copies:
        copy.start()
    return copies


def finish(copies):
    for copy in copies:
        copy.wait()


def split(value):
    high = value.astype(BF)
    return high, (value - high.astype(F32)).astype(BF)


def dot(left, right):
    return jnp.dot(left, right, preferred_element_type=F32)


CHUNK = 16


def chunks():
    return [slice(i, i + CHUNK) for i in range(0, R, CHUNK)]


def put_column(ref, case, rows, value):
    high, low = split(value)
    size = ref.shape[-2] // 3
    lanes = slice(case % 2 * R, (case % 2 + 1) * R)
    for place, part in enumerate((high, high, low)):
        ref[case // 2, rows.start + place * size : rows.stop + place * size, lanes] = part


def put_row(ref, first, rows, left, right):
    rows = slice(first + rows.start, first + rows.stop)
    for third, value in enumerate((left + right, left, right)):
        high, low = split(value)
        for place, part in enumerate((high, low, high)):
            ref[rows, (3 * third + place) * R : (3 * third + place + 1) * R] = part


def inner_stage(mid_ref, row_ref, inner_ref, every):
    for third in range(3):
        mid_ref[every, third * R : (third + 1) * R] = dot(
            row_ref[every, 3 * third * R : 3 * (third + 1) * R], inner_ref[third]
        )


def inner_parts(mid_ref, here):
    common = mid_ref[here, 0:R]
    return common + mid_ref[here, 2 * R : 3 * R], common + mid_ref[here, R : 2 * R]


def outer_stage(pair, column_ref, first_ref, outer_ref, turn_ref, row_ref):
    first_ref[...] = dot(outer_ref[...], column_ref[pair])
    for side in range(2):
        lanes = slice(side * R, (side + 1) * R)
        for rows in chunks():
            real, imag = first_ref[rows, lanes], first_ref[R + rows.start : R + rows.stop, lanes]
            turn_real, turn_imag = turn_ref[0, rows, :], turn_ref[1, rows, :]
            put_row(
                row_ref,
                (2 * pair + side) * R,
                rows,
                real * turn_real - imag * turn_imag,
                real * turn_imag + imag * turn_real,
            )


def taps_columns(taps_ref, column_ref):
    taps = jnp.concatenate([taps_ref[j] for j in range(3)], axis=0)
    padded = jnp.concatenate([taps, jnp.zeros((7, taps.shape[1]), F32)], axis=0)
    column_ref[:, 0:16] = padded.T


def gate_kernel(length_ref, taps_hbm, features_ref, out_ref, taps_ref, column_ref, in_ref, send_ref, in_sem, out_sem):
    taps_copy = pltpu.make_async_copy(taps_hbm, taps_ref, in_sem.at[in_ref.shape[0]])
    taps_copy.start()
    width = features_ref.shape[3]
    parts = in_ref.shape[0]
    group = in_ref.shape[2]
    copies = [
        pltpu.make_async_copy(
            features_ref.at[0, pl.ds(1, 2), pl.ds(group * part, group), :], in_ref.at[part], in_sem.at[part]
        )
        for part in range(parts)
    ]
    for copy in copies:
        copy.start()
    taps_copy.wait()
    taps_columns(taps_ref, column_ref)
    limit = length_ref[...].reshape(1, 1) - lax.axis_index("seq") * width
    near = lax.broadcasted_iota(jnp.int32, (8, 128), 1)
    sends = []
    for part in range(parts):
        copies[part].wait()
        for sub in range(group // 8):
            channel = part * group + sub * 8
            column = column_ref[channel : channel + 8, :]

            tap = [[jnp.broadcast_to(column[:, 3 * j + i : 3 * j + i + 1], (8, 128)) for i in range(3)] for j in (1, 2)]

            def tile_of(j, tile):
                lanes = slice(tile * 128, tile * 128 + 128)
                return in_ref[part, j, sub * 8 : sub * 8 + 8, lanes]

            last = width // 128 - 1
            before = [tile_of(j, last) for j in range(2)]
            turned = [[pltpu.roll(before[j], i, 1) for i in (1, 2)] for j in range(2)]
            over = [
                tap[j][1] * jnp.where(near < 1, turned[j][0], 0.0) + tap[j][2] * jnp.where(near < 2, turned[j][1], 0.0)
                for j in range(2)
            ]
            turned = [[jnp.zeros((8, 128), F32)] * 2] * 2
            for tile in range(width // 128):
                values = []
                for j in range(2):
                    here = tile_of(j, tile)
                    one, two = pltpu.roll(here, 1, 1), pltpu.roll(here, 2, 1)
                    values.append(
                        tap[j][0] * here
                        + tap[j][1] * jnp.where(near < 1, turned[j][0], one)
                        + tap[j][2] * jnp.where(near < 2, turned[j][1], two)
                    )
                    turned = [turned[i] if i != j else [one, two] for i in range(2)]
                if tile == 0:
                    key, value = values
                row = channel * SPAN + (tile % 2) * 16 + tile // 2
                send_ref[pl.ds(row, 8, stride=SPAN), :] = jnp.where(
                    near + tile * 128 < limit, values[0] * values[1], 0.0
                )
            key_over, value_over = over
            flag = jnp.where(near < limit, 1.0, 0.0)
            edge = jnp.where(near < 2, key, 0.0)
            for place, item in ((1, value), (2, key_over), (3, value_over), (4, flag)):
                inside = (near >= 2 * place) & (near < 2 * place + 2)
                edge = jnp.where(inside, pltpu.roll(item, 2 * place, 1), edge)
            send_ref[pl.ds(channel * SPAN + 32, 8, stride=SPAN), :] = edge
        rows = pl.ds(part * group * SPAN, group * SPAN)
        there = pl.ds(part * group * SPAN, group * SPAN)
        send = pltpu.make_async_copy(send_ref.at[rows, :], out_ref.at[there, :], out_sem.at[part])
        send.start()
        sends.append(send)
    for send in sends:
        send.wait()


def gate(lengths, short_filter, features):
    _, _, channels, width = features.shape
    parts = 4
    return pl.pallas_call(
        gate_kernel,
        in_specs=[VM, HB, HB],
        out_specs=HB,
        out_shape=jax.ShapeDtypeStruct((channels * SPAN, 128), F32),
        scratch_shapes=[
            pltpu.VMEM(short_filter.shape, F32),
            pltpu.VMEM((channels, 128), F32),
            pltpu.VMEM((parts, 2, channels // parts, width), F32),
            pltpu.VMEM((channels * SPAN, 128), F32),
            pltpu.SemaphoreType.DMA((parts + 1,)),
            pltpu.SemaphoreType.DMA((parts,)),
        ],
        compiler_params=pltpu.CompilerParams(vmem_limit_bytes=60 << 20),
        cost_estimate=pl.CostEstimate(flops=1 << 20, bytes_accessed=12 << 20, transcendentals=0),
        name="gate",
    )(lengths, short_filter, features)


def pair_kernel(mine_ref, other_ref, out_ref):
    x = lax.axis_index("x_lo")
    mine = jnp.where(x == 0, mine_ref[0:2, :], mine_ref[2:4, :])
    other = jnp.where(x == 0, other_ref[0:2, :], other_ref[2:4, :])
    parts = (jnp.where(x == 0, mine, other), jnp.where(x == 0, other, mine))
    for channel in range(2):
        for place in range(2):
            for row in range(32):
                out_ref[channel, place, row : row + 1, :] = parts[place][
                    channel : channel + 1, row * R : row * R + R
                ]


def pair_up(mine, other):
    return pl.pallas_call(
        pair_kernel,
        in_specs=[VM, VM],
        out_specs=VM,
        out_shape=jax.ShapeDtypeStruct((2, 2, 32, R), F32),
        compiler_params=pltpu.CompilerParams(vmem_limit_bytes=4 << 20),
        name="pair_up",
    )(mine, other)


def filter_kernel(
    skip_ref,
    p0,
    p1,
    p2,
    p3,
    table_hbm,
    turn_hbm,
    spec_hbm,
    turn_ref,
    column_ref,
    first_ref,
    row_ref,
    mid_ref,
    spec_ref,
    outer_ref,
    inner_ref,
    sem,
):
    outer_copies = start(load_outer(table_hbm, outer_ref, sem.at[0]))
    turn_copies = start([pltpu.make_async_copy(turn_hbm, turn_ref, sem.at[1])])
    inner_copies = start(load_inner(table_hbm, inner_ref, sem.at[2:4]))
    y, x = lax.axis_index("y"), lax.axis_index("x_lo")
    for away, part in enumerate((p0, p1, p2, p3)):
        first = lax.rem(y + 4 - away, 4) * 64
        for channel in range(2):
            for place in range(2):
                for half in range(2):
                    high, low = split(part[channel, place, 16 * half : 16 * half + 16, :])
                    for third, piece in enumerate((high, high, low)):
                        at = pl.multiple_of(third * R + first + 32 * place + 16 * half, 16)
                        column_ref[0, pl.ds(at, 16), channel * R : (channel + 1) * R] = piece
    finish(outer_copies + turn_copies)
    repeat_lanes(outer_ref, 2 * R, R)
    outer_stage(0, column_ref, first_ref, outer_ref, turn_ref, row_ref)
    finish(inner_copies)
    repeat_inner(inner_ref)
    sends = []
    for channel in range(2):
        inner_stage(mid_ref, row_ref, inner_ref, slice(channel * R, (channel + 1) * R))
        skip = skip_ref[2 * x + channel]
        for rows in chunks():
            real, imag = inner_parts(mid_ref, slice(channel * R + rows.start, channel * R + rows.stop))
            spec_ref[channel, 0, rows, :] = (real + skip) * (1.0 / N)
            spec_ref[channel, 1, rows, :] = imag * (1.0 / N)
        sends += start(
            [pltpu.make_async_copy(spec_ref.at[channel], spec_hbm.at[channel], sem.at[4 + channel])]
        )
    finish(sends)


def filter_spectrum(skip_gain, parts, table, turn):
    return pl.pallas_call(
        filter_kernel,
        in_specs=[SM] + [VM] * 4 + [HB] * 2,
        out_specs=HB,
        out_shape=jax.ShapeDtypeStruct((2, 2, R, R), F32),
        scratch_shapes=[
            pltpu.VMEM(turn.shape, F32),
            pltpu.VMEM((1, 3 * R, 2 * R), BF),
            pltpu.VMEM((2 * R, 2 * R), F32),
            pltpu.VMEM((2 * R, 9 * R), BF),
            pltpu.VMEM((2 * R, 3 * R), F32),
            pltpu.VMEM((2, 2, R, R), F32),
            pltpu.VMEM(*TABLES[0]),
            pltpu.VMEM(*TABLES[2]),
            pltpu.SemaphoreType.DMA((6,)),
        ],
        compiler_params=pltpu.CompilerParams(vmem_limit_bytes=40 << 20),
        name="filter_spectrum",
    )(skip_gain, *parts, table, turn)


def conv_kernel(
    moved_hbm,
    spec_hbm,
    turn_hbm,
    table_hbm,
    out_hbm,
    moved_ref,
    spec_ref,
    turn_ref,
    column_ref,
    first_ref,
    row_ref,
    mid_ref,
    last_ref,
    result_ref,
    outer_ref,
    back_ref,
    inner_ref,
    sem,
    out_sem,
):
    cut = 40
    moved_copies = [
        pltpu.make_async_copy(moved_hbm.at[:, rows, :], moved_ref.at[:, rows, :], sem.at[i])
        for i, rows in enumerate((slice(0, cut), slice(cut, 2 * SPAN)))
    ]
    start(moved_copies[0:1])
    outer_copies = start(load_outer(table_hbm, outer_ref, sem.at[2]))
    turn_copies = start([pltpu.make_async_copy(turn_hbm, turn_ref, sem.at[3])])
    start(moved_copies[1:2])
    inner_copies = start(load_inner(table_hbm, inner_ref, sem.at[4:6]))
    spec_copies = start([pltpu.make_async_copy(spec_hbm, spec_ref, sem.at[6])])
    back_copies = start(load_back(table_hbm, back_ref, sem.at[7:9]))
    blocks = N // 4096
    lane = lax.broadcasted_iota(jnp.int32, (blocks, 128), 1)
    block = lax.broadcasted_iota(jnp.int32, (blocks, 128), 0)
    for channel in range(2):
        finish(moved_copies[0:1] if channel == 0 else moved_copies[1:2] + inner_copies + spec_copies + back_copies)
        if channel == 1:
            repeat_inner(inner_ref)
            repeat_lanes(back_ref, 4 * R, 2 * R)
        begin = channel * SPAN
        for rep in range(2):
            case = 2 * channel + rep
            edge = jnp.concatenate(
                [moved_ref[2 * b + rep, begin + 32 : begin + 33, :] for b in range(blocks)], axis=0
            )
            behind = jnp.where(block < 1, 0.0, pltpu.roll(edge, 1, 0))
            key = edge + pltpu.roll(behind, 124, 1)
            value = pltpu.roll(edge, 126, 1) + pltpu.roll(behind, 122, 1)
            mended = key * value * pltpu.roll(edge, 120, 1)
            for b in range(blocks):
                left = moved_ref[2 * b + rep, begin : begin + 16, :]
                right = moved_ref[2 * b + rep, begin + 16 : begin + 32, :]
                left = jnp.where((block < 1) & (lane < 2), mended[b : b + 1], left)
                put_column(
                    column_ref, case, slice(16 * b, 16 * b + 16), jnp.concatenate([left, right], axis=1)
                )
        if channel == 0:
            finish(outer_copies + turn_copies)
            repeat_lanes(outer_ref, 2 * R, R)
        outer_stage(channel, column_ref, first_ref.at[channel], outer_ref, turn_ref, row_ref)
    sends = []
    size = 2 * R
    def forward_inner(group):
        every = slice(group * size, (group + 1) * size)
        inner_stage(mid_ref, row_ref, inner_ref, every)

    def multiply(group):
        for case in range(2 * group, 2 * group + 2):
            channel = case // 2
            for rows in chunks():
                here = slice(case * R + rows.start, case * R + rows.stop)
                real, imag = inner_parts(mid_ref, here)
                spec_real, spec_imag = spec_ref[channel, 0, rows, :], spec_ref[channel, 1, rows, :]
                put_row(
                    row_ref,
                    case * R,
                    rows,
                    real * spec_imag + imag * spec_real,
                    real * spec_real - imag * spec_imag,
                )

    def untwist(group):
        for case in range(2 * group, 2 * group + 2):
            for rows in chunks():
                here = slice(case * R + rows.start, case * R + rows.stop)
                imag, real = inner_parts(mid_ref, here)
                turn_real, turn_imag = turn_ref[0, rows, :], turn_ref[1, rows, :]
                put_column(last_ref, case, rows, real * turn_real + imag * turn_imag)
                below = slice(R + rows.start, R + rows.stop)
                put_column(last_ref, case, below, imag * turn_real - real * turn_imag)

    def backward_outer(group):
        result = dot(back_ref[...], last_ref[group])
        for rep in range(2):
            for half in range(2):
                lanes = slice(rep * R + half * 128, rep * R + half * 128 + 128)
                result_ref[group, rep, :, half * 16 : half * 16 + 16, :] = result[:, lanes].reshape(
                    blocks, 16, 128
                )
            sends.extend(
                start(
                    [
                        pltpu.make_async_copy(
                            result_ref.at[group, rep],
                            out_hbm.reshape(16, 2, 64, 128).at[:, rep, pl.ds(group * 32, 32), :],
                            out_sem.at[2 * group + rep],
                        )
                    ]
                )
            )

    stages = (forward_inner, multiply, forward_inner, untwist, backward_outer)
    groups = 2
    for step in range(len(stages) + groups - 1):
        for group in range(groups):
            if 0 <= step - group < len(stages):
                stages[step - group](group)
    finish(sends)


def convolve(moved, spec, turn, table):
    return pl.pallas_call(
        conv_kernel,
        in_specs=[HB] * 4,
        out_specs=HB,
        out_shape=jax.ShapeDtypeStruct((32, 64, 128), F32),
        scratch_shapes=[
            pltpu.VMEM(moved.shape, F32),
            pltpu.VMEM(spec.shape, F32),
            pltpu.VMEM(turn.shape, F32),
            pltpu.VMEM((2, 3 * R, 2 * R), BF),
            pltpu.VMEM((2, 2 * R, 2 * R), F32),
            pltpu.VMEM((4 * R, 9 * R), BF),
            pltpu.VMEM((4 * R, 3 * R), F32),
            pltpu.VMEM((2, 6 * R, 2 * R), BF),
            pltpu.VMEM((2, 2, 16, 32, 128), F32),
        ]
        + [pltpu.VMEM(*table_like) for table_like in TABLES]
        + [pltpu.SemaphoreType.DMA((9,)), pltpu.SemaphoreType.DMA((4,))],
        compiler_params=pltpu.CompilerParams(vmem_limit_bytes=60 << 20),
        name="convolve",
    )(moved, spec, turn, table)


def query_kernel(length_hbm, taps_ref, features_ref, out_ref, edge_ref, length_ref, column_ref, sem):
    group, width = out_ref.shape

    @pl.when(pl.program_id(0) == 0)
    def _():
        finish(start([pltpu.make_async_copy(length_hbm, length_ref, sem)]))
        taps_columns(taps_ref, column_ref)

    limit = length_ref[0] - lax.axis_index("seq") * width
    lane = lax.broadcasted_iota(jnp.int32, (8, width), 1)
    near = lane[:, 0:128]
    for sub in range(group // 8):
        rows = pl.ds(pl.multiple_of(pl.program_id(0) * group + sub * 8, 8), 8)
        column = column_ref[rows, :]
        here = features_ref[sub * 8 : sub * 8 + 8, :]
        t0, t1, t2 = (column[:, i : i + 1] for i in range(3))
        one = jnp.where(lane < 1, 0.0, pltpu.roll(here, 1, 1))
        two = jnp.where(lane < 2, 0.0, pltpu.roll(here, 2, 1))
        value = t0 * here + t1 * one + t2 * two
        out_ref[sub * 8 : sub * 8 + 8, :] = jnp.where(lane < limit, value, 0.0)
        here = slice(sub * 8, sub * 8 + 8)
        edge_ref[here, 0:128] = jnp.where((near < 1) & (near < limit), t1, 0.0)
        edge_ref[here, 128:256] = jnp.where((near < 2) & (near < limit), t2, 0.0)


def query(lengths, short_filter, features):
    _, streams, channels, width = features.shape
    group = 16
    return pl.pallas_call(
        query_kernel,
        grid=(channels // group,),
        in_specs=[HB, VM, pl.BlockSpec((None, None, group, width), lambda i: (0, 0, i, 0))],
        out_specs=[
            pl.BlockSpec((group, width), lambda i: (i, 0)),
            pl.BlockSpec((group, 256), lambda i: (i, 0)),
        ],
        out_shape=[
            jax.ShapeDtypeStruct((channels, width), F32),
            jax.ShapeDtypeStruct((channels, 256), F32),
        ],
        scratch_shapes=[
            pltpu.SMEM((1,), jnp.int32),
            pltpu.VMEM((channels, 128), F32),
            pltpu.SemaphoreType.DMA,
        ],
        compiler_params=pltpu.CompilerParams(vmem_limit_bytes=12 << 20),
        name="query",
    )(lengths, short_filter, features)


def mix_kernel(
    query_hbm, edge_hbm, tail_hbm, back_hbm, out_hbm, query_ref, edge_ref, tail_ref, back_ref, out_ref, sem
):
    channels, width = out_ref.shape
    parts = 4
    group = channels // parts
    small = start(
        [
            pltpu.make_async_copy(edge_hbm, edge_ref, sem.at[3, 0]),
            pltpu.make_async_copy(tail_hbm, tail_ref, sem.at[3, 1]),
        ]
    )
    loads = []
    for part in range(parts):
        rows, there = pl.ds(group * part, group), pl.ds(32 * group * part, 32 * group)
        loads.append(
            start(
                [
                    pltpu.make_async_copy(query_hbm.at[rows, :], query_ref.at[rows, :], sem.at[0, part]),
                    pltpu.make_async_copy(back_hbm.at[there, :], back_ref.at[there, :], sem.at[1, part]),
                ]
            )
        )
    finish(small)
    sends = []
    for part in range(parts):
        finish(loads[part])
        for sub in range(group // 8):
            channel = part * group + sub * 8
            here = slice(channel, channel + 8)
            tail = tail_ref[here, :]
            mend = pltpu.roll(tail, 1, 1) * edge_ref[here, 0:128] + pltpu.roll(tail, 2, 1) * edge_ref[here, 128:256]
            for tile in range(width // 128):
                row = channel * 32 + (tile % 2) * 16 + tile // 2
                lanes = slice(tile * 128, tile * 128 + 128)
                value = query_ref[here, lanes]
                if tile == 0:
                    value = value + mend
                out_ref[here, lanes] = value * back_ref[pl.ds(row, 8, stride=32), :]
        rows = pl.ds(group * part, group)
        sends += start([pltpu.make_async_copy(out_ref.at[rows, :], out_hbm.at[0, rows, :], sem.at[2, part])])
    finish(sends)


def mix(query, edge, tail, returned):
    return pl.pallas_call(
        mix_kernel,
        in_specs=[HB] * 4,
        out_specs=HB,
        out_shape=jax.ShapeDtypeStruct((1,) + query.shape, F32),
        scratch_shapes=[
            pltpu.VMEM(query.shape, F32),
            pltpu.VMEM(edge.shape, F32),
            pltpu.VMEM(tail.shape, F32),
            pltpu.VMEM(returned.shape, F32),
            pltpu.VMEM(query.shape, F32),
            pltpu.SemaphoreType.DMA((4, 4)),
        ],
        compiler_params=pltpu.CompilerParams(vmem_limit_bytes=60 << 20),
        name="mix",
    )(query, edge, tail, returned)


def exchange(blocks):
    return lax.all_to_all(blocks, ("seq", "x_lo"), split_axis=0, concat_axis=0, tiled=True)


def body(features, short_filter, long_filter, skip_gain, lengths):
    seq_dev = features.shape[3]
    n_seq = lax.axis_size("seq")
    table, turn = (jnp.asarray(t) for t in tables())
    other = lax.ppermute(long_filter, "x_lo", [(0, 1), (1, 0)])
    gated = gate(lengths, short_filter, features)
    gated, other = lax.optimization_barrier((gated, other))
    moved = exchange(gated.reshape(2 * n_seq, 2 * SPAN, 128))
    pair = pair_up(long_filter, other)
    parts = [pair] + [
        lax.ppermute(pair, "y", [(i, (i + away) % 4) for i in range(4)]) for away in range(1, 4)
    ]
    spec = filter_spectrum(skip_gain, parts, table, turn)
    convolved = convolve(moved, spec, turn, table)
    returned = exchange(convolved)
    tail = lax.ppermute(features[0, 0, :, seq_dev - 128 :], "seq", [(i, i + 1) for i in range(n_seq - 1)])
    gates, edge = query(lengths, short_filter, features)
    return mix(gates, edge, tail, returned.reshape(2 * n_seq * 64, 128))


def solution(mesh):
    devices = mesh.devices
    reps, seqs = devices.shape
    finer = Mesh(devices.reshape(reps // 2, 2, seqs), ("y", "x_lo", "seq"))
    rep = ("y", "x_lo")
    return jax.shard_map(
        body,
        mesh=finer,
        in_specs=(P(rep, None, None, "seq"), P(), P("seq", rep), P("seq"), P(rep)),
        out_specs=P(rep, None, "seq"),
        check_vma=False,
    )
```

```python
import math

import jax
import jax.numpy as jnp
import ml_dtypes
import numpy as np
from jax import lax
from jax.experimental import pallas as pl
from jax.experimental.pallas import tpu as pltpu
from jax.sharding import Mesh
from jax.sharding import PartitionSpec as P

R = 256
N = R * R
BF = jnp.bfloat16
F32 = jnp.float32
SPAN = 36

VM = pl.BlockSpec(memory_space=pltpu.VMEM)
SM = pl.BlockSpec(memory_space=pltpu.SMEM)
HB = pl.BlockSpec(memory_space=pltpu.HBM)


def halves(table, axis):
    high = table.astype(np.float32).astype(ml_dtypes.bfloat16)
    low = (table - high.astype(np.float64)).astype(np.float32).astype(ml_dtypes.bfloat16)
    return np.concatenate([high, low], axis=axis)


def tables():
    row = np.arange(R, dtype=np.float64)
    first = 2.0 * math.pi / R * np.outer(row + 0.25, row)
    outer = np.concatenate([np.cos(first), -np.sin(first)], axis=0)
    twist = 2.0 * math.pi / N * np.outer(row + 0.25, row)
    turn = np.stack([np.cos(twist), -np.sin(twist)]).astype(np.float32)
    last = 2.0 * math.pi / R * np.outer(row, row)
    cos, sin = np.cos(last), -np.sin(last)
    inner = np.concatenate([cos, sin - cos, -cos - sin], axis=0)
    return np.concatenate([halves(outer, 1), halves(outer.T, 0), halves(inner, 1)], axis=0), turn


TABLES = (
    ((2 * R, 3 * R), BF),
    ((R, 6 * R), BF),
    ((3, 3 * R, R), BF),
)


def load_outer(table_hbm, outer_ref, sem):
    return [pltpu.make_async_copy(table_hbm.at[0 : 2 * R, :], outer_ref.at[:, 0 : 2 * R], sem)]


def load_back(table_hbm, back_ref, sem):
    return [
        pltpu.make_async_copy(
            table_hbm.at[(2 + i) * R : (3 + i) * R, :], back_ref.at[:, 2 * R * i : 2 * R * (i + 1)], sem.at[i]
        )
        for i in range(2)
    ]


def load_inner(table_hbm, inner_ref, sem):
    stack = table_hbm.reshape(7, R, 2 * R)
    return [
        pltpu.make_async_copy(
            stack.at[4:7, :, i * R : (i + 1) * R], inner_ref.at[:, (i + 1) * R : (i + 2) * R, :], sem.at[i]
        )
        for i in range(2)
    ]


def repeat_inner(ref):
    for third in range(3):
        for i in range(0, R, 64):
            ref[third, i : i + 64, :] = ref[third, R + i : R + i + 64, :]


def repeat_lanes(ref, target, count):
    for i in range(0, ref.shape[0], 64):
        ref[i : i + 64, target : target + count] = ref[i : i + 64, 0:count]


def start(copies):
    for copy in copies:
        copy.start()
    return copies


def finish(copies):
    for copy in copies:
        copy.wait()


def split(value):
    high = value.astype(BF)
    return high, (value - high.astype(F32)).astype(BF)


def dot(left, right):
    return jnp.dot(left, right, preferred_element_type=F32)


CHUNK = 16


def chunks():
    return [slice(i, i + CHUNK) for i in range(0, R, CHUNK)]


def put_column(ref, case, rows, value):
    high, low = split(value)
    size = ref.shape[-2] // 3
    lanes = slice(case % 2 * R, (case % 2 + 1) * R)
    for place, part in enumerate((high, high, low)):
        ref[case // 2, rows.start + place * size : rows.stop + place * size, lanes] = part


def put_row(ref, first, rows, left, right):
    rows = slice(first + rows.start, first + rows.stop)
    for third, value in enumerate((left + right, left, right)):
        high, low = split(value)
        for place, part in enumerate((high, low, high)):
            ref[rows, (3 * third + place) * R : (3 * third + place + 1) * R] = part


def inner_stage(mid_ref, row_ref, inner_ref, every):
    for third in range(3):
        mid_ref[every, third * R : (third + 1) * R] = dot(
            row_ref[every, 3 * third * R : 3 * (third + 1) * R], inner_ref[third]
        )


def inner_parts(mid_ref, here):
    common = mid_ref[here, 0:R]
    return common + mid_ref[here, 2 * R : 3 * R], common + mid_ref[here, R : 2 * R]


def outer_stage(pair, column_ref, first_ref, outer_ref, turn_ref, row_ref):
    first_ref[...] = dot(outer_ref[...], column_ref[pair])
    for side in range(2):
        lanes = slice(side * R, (side + 1) * R)
        for rows in chunks():
            real, imag = first_ref[rows, lanes], first_ref[R + rows.start : R + rows.stop, lanes]
            turn_real, turn_imag = turn_ref[0, rows, :], turn_ref[1, rows, :]
            put_row(
                row_ref,
                (2 * pair + side) * R,
                rows,
                real * turn_real - imag * turn_imag,
                real * turn_imag + imag * turn_real,
            )


def taps_columns(taps_ref, column_ref):
    taps = jnp.concatenate([taps_ref[j] for j in range(3)], axis=0)
    padded = jnp.concatenate([taps, jnp.zeros((7, taps.shape[1]), F32)], axis=0)
    column_ref[:, 0:16] = padded.T


def gate_kernel(length_ref, taps_hbm, features_ref, out_ref, taps_ref, column_ref, in_ref, send_ref, in_sem, out_sem):
    taps_copy = pltpu.make_async_copy(taps_hbm, taps_ref, in_sem.at[in_ref.shape[0]])
    taps_copy.start()
    width = features_ref.shape[3]
    parts = in_ref.shape[0]
    group = in_ref.shape[2]
    copies = [
        pltpu.make_async_copy(
            features_ref.at[0, pl.ds(1, 2), pl.ds(group * part, group), :], in_ref.at[part], in_sem.at[part]
        )
        for part in range(parts)
    ]
    for copy in copies:
        copy.start()
    taps_copy.wait()
    taps_columns(taps_ref, column_ref)
    limit = length_ref[...].reshape(1, 1) - lax.axis_index("seq") * width
    near = lax.broadcasted_iota(jnp.int32, (8, 128), 1)
    sends = []
    for part in range(parts):
        copies[part].wait()
        for sub in range(group // 8):
            channel = part * group + sub * 8
            column = column_ref[channel : channel + 8, :]

            tap = [[jnp.broadcast_to(column[:, 3 * j + i : 3 * j + i + 1], (8, 128)) for i in range(3)] for j in (1, 2)]

            def tile_of(j, tile):
                lanes = slice(tile * 128, tile * 128 + 128)
                return in_ref[part, j, sub * 8 : sub * 8 + 8, lanes]

            last = width // 128 - 1
            before = [tile_of(j, last) for j in range(2)]
            turned = [[pltpu.roll(before[j], i, 1) for i in (1, 2)] for j in range(2)]
            over = [
                tap[j][1] * jnp.where(near < 1, turned[j][0], 0.0) + tap[j][2] * jnp.where(near < 2, turned[j][1], 0.0)
                for j in range(2)
            ]
            turned = [[jnp.zeros((8, 128), F32)] * 2] * 2
            for tile in range(width // 128):
                values = []
                for j in range(2):
                    here = tile_of(j, tile)
                    one, two = pltpu.roll(here, 1, 1), pltpu.roll(here, 2, 1)
                    values.append(
                        tap[j][0] * here
                        + tap[j][1] * jnp.where(near < 1, turned[j][0], one)
                        + tap[j][2] * jnp.where(near < 2, turned[j][1], two)
                    )
                    turned = [turned[i] if i != j else [one, two] for i in range(2)]
                if tile == 0:
                    key, value = values
                row = channel * SPAN + (tile % 2) * 16 + tile // 2
                send_ref[pl.ds(row, 8, stride=SPAN), :] = jnp.where(
                    near + tile * 128 < limit, values[0] * values[1], 0.0
                )
            key_over, value_over = over
            flag = jnp.where(near < limit, 1.0, 0.0)
            edge = jnp.where(near < 2, key, 0.0)
            for place, item in ((1, value), (2, key_over), (3, value_over), (4, flag)):
                inside = (near >= 2 * place) & (near < 2 * place + 2)
                edge = jnp.where(inside, pltpu.roll(item, 2 * place, 1), edge)
            send_ref[pl.ds(channel * SPAN + 32, 8, stride=SPAN), :] = edge
        rows = pl.ds(part * group * SPAN, group * SPAN)
        there = pl.ds(part * group * SPAN, group * SPAN)
        send = pltpu.make_async_copy(send_ref.at[rows, :], out_ref.at[there, :], out_sem.at[part])
        send.start()
        sends.append(send)
    for send in sends:
        send.wait()


def gate(lengths, short_filter, features):
    _, _, channels, width = features.shape
    parts = 4
    return pl.pallas_call(
        gate_kernel,
        in_specs=[VM, HB, HB],
        out_specs=HB,
        out_shape=jax.ShapeDtypeStruct((channels * SPAN, 128), F32),
        scratch_shapes=[
            pltpu.VMEM(short_filter.shape, F32),
            pltpu.VMEM((channels, 128), F32),
            pltpu.VMEM((parts, 2, channels // parts, width), F32),
            pltpu.VMEM((channels * SPAN, 128), F32),
            pltpu.SemaphoreType.DMA((parts + 1,)),
            pltpu.SemaphoreType.DMA((parts,)),
        ],
        compiler_params=pltpu.CompilerParams(vmem_limit_bytes=60 << 20),
        cost_estimate=pl.CostEstimate(flops=1 << 20, bytes_accessed=12 << 20, transcendentals=0),
        name="gate",
    )(lengths, short_filter, features)


def pair_kernel(mine_ref, other_ref, out_ref):
    x = lax.axis_index("x_lo")
    mine = jnp.where(x == 0, mine_ref[0:2, :], mine_ref[2:4, :])
    other = jnp.where(x == 0, other_ref[0:2, :], other_ref[2:4, :])
    parts = (jnp.where(x == 0, mine, other), jnp.where(x == 0, other, mine))
    for channel in range(2):
        for place in range(2):
            for row in range(32):
                out_ref[channel, place, row : row + 1, :] = parts[place][
                    channel : channel + 1, row * R : row * R + R
                ]


def pair_up(mine, other):
    return pl.pallas_call(
        pair_kernel,
        in_specs=[VM, VM],
        out_specs=VM,
        out_shape=jax.ShapeDtypeStruct((2, 2, 32, R), F32),
        compiler_params=pltpu.CompilerParams(vmem_limit_bytes=4 << 20),
        name="pair_up",
    )(mine, other)


def filter_kernel(
    skip_ref,
    p0,
    p1,
    p2,
    p3,
    table_hbm,
    turn_hbm,
    spec_hbm,
    turn_ref,
    column_ref,
    first_ref,
    row_ref,
    mid_ref,
    spec_ref,
    outer_ref,
    inner_ref,
    sem,
):
    outer_copies = start(load_outer(table_hbm, outer_ref, sem.at[0]))
    turn_copies = start([pltpu.make_async_copy(turn_hbm, turn_ref, sem.at[1])])
    inner_copies = start(load_inner(table_hbm, inner_ref, sem.at[2:4]))
    y, x = lax.axis_index("y"), lax.axis_index("x_lo")
    for away, part in enumerate((p0, p1, p2, p3)):
        first = lax.rem(y + 4 - away, 4) * 64
        for channel in range(2):
            for place in range(2):
                for half in range(2):
                    high, low = split(part[channel, place, 16 * half : 16 * half + 16, :])
                    for third, piece in enumerate((high, high, low)):
                        at = pl.multiple_of(third * R + first + 32 * place + 16 * half, 16)
                        column_ref[0, pl.ds(at, 16), channel * R : (channel + 1) * R] = piece
    finish(outer_copies + turn_copies)
    repeat_lanes(outer_ref, 2 * R, R)
    outer_stage(0, column_ref, first_ref, outer_ref, turn_ref, row_ref)
    finish(inner_copies)
    repeat_inner(inner_ref)
    sends = []
    for channel in range(2):
        inner_stage(mid_ref, row_ref, inner_ref, slice(channel * R, (channel + 1) * R))
        skip = skip_ref[2 * x + channel]
        for rows in chunks():
            real, imag = inner_parts(mid_ref, slice(channel * R + rows.start, channel * R + rows.stop))
            spec_ref[channel, 0, rows, :] = (real + skip) * (1.0 / N)
            spec_ref[channel, 1, rows, :] = imag * (1.0 / N)
        sends += start(
            [pltpu.make_async_copy(spec_ref.at[channel], spec_hbm.at[channel], sem.at[4 + channel])]
        )
    finish(sends)


def filter_spectrum(skip_gain, parts, table, turn):
    return pl.pallas_call(
        filter_kernel,
        in_specs=[SM] + [VM] * 4 + [HB] * 2,
        out_specs=HB,
        out_shape=jax.ShapeDtypeStruct((2, 2, R, R), F32),
        scratch_shapes=[
            pltpu.VMEM(turn.shape, F32),
            pltpu.VMEM((1, 3 * R, 2 * R), BF),
            pltpu.VMEM((2 * R, 2 * R), F32),
            pltpu.VMEM((2 * R, 9 * R), BF),
            pltpu.VMEM((2 * R, 3 * R), F32),
            pltpu.VMEM((2, 2, R, R), F32),
            pltpu.VMEM(*TABLES[0]),
            pltpu.VMEM(*TABLES[2]),
            pltpu.SemaphoreType.DMA((6,)),
        ],
        compiler_params=pltpu.CompilerParams(vmem_limit_bytes=40 << 20),
        name="filter_spectrum",
    )(skip_gain, *parts, table, turn)


def conv_kernel(
    moved_hbm,
    spec_hbm,
    turn_hbm,
    table_hbm,
    out_hbm,
    moved_ref,
    spec_ref,
    turn_ref,
    column_ref,
    first_ref,
    row_ref,
    mid_ref,
    last_ref,
    result_ref,
    outer_ref,
    back_ref,
    inner_ref,
    sem,
    out_sem,
):
    cut = 40
    moved_copies = [
        pltpu.make_async_copy(moved_hbm.at[:, rows, :], moved_ref.at[:, rows, :], sem.at[i])
        for i, rows in enumerate((slice(0, cut), slice(cut, 2 * SPAN)))
    ]
    outer_copies = start(load_outer(table_hbm, outer_ref, sem.at[2]))
    start(moved_copies[0:1])
    turn_copies = start([pltpu.make_async_copy(turn_hbm, turn_ref, sem.at[3])])
    start(moved_copies[1:2])
    inner_copies = start(load_inner(table_hbm, inner_ref, sem.at[4:6]))
    spec_copies = start([pltpu.make_async_copy(spec_hbm, spec_ref, sem.at[6])])
    back_copies = start(load_back(table_hbm, back_ref, sem.at[7:9]))
    blocks = N // 4096
    lane = lax.broadcasted_iota(jnp.int32, (blocks, 128), 1)
    block = lax.broadcasted_iota(jnp.int32, (blocks, 128), 0)
    for channel in range(2):
        finish(moved_copies[0:1] if channel == 0 else moved_copies[1:2] + inner_copies + spec_copies + back_copies)
        if channel == 1:
            repeat_inner(inner_ref)
            repeat_lanes(back_ref, 4 * R, 2 * R)
        begin = channel * SPAN
        for rep in range(2):
            case = 2 * channel + rep
            edge = jnp.concatenate(
                [moved_ref[2 * b + rep, begin + 32 : begin + 33, :] for b in range(blocks)], axis=0
            )
            behind = jnp.where(block < 1, 0.0, pltpu.roll(edge, 1, 0))
            key = edge + pltpu.roll(behind, 124, 1)
            value = pltpu.roll(edge, 126, 1) + pltpu.roll(behind, 122, 1)
            mended = key * value * pltpu.roll(edge, 120, 1)
            for b in range(blocks):
                left = moved_ref[2 * b + rep, begin : begin + 16, :]
                right = moved_ref[2 * b + rep, begin + 16 : begin + 32, :]
                left = jnp.where((block < 1) & (lane < 2), mended[b : b + 1], left)
                put_column(
                    column_ref, case, slice(16 * b, 16 * b + 16), jnp.concatenate([left, right], axis=1)
                )
        if channel == 0:
            finish(outer_copies + turn_copies)
            repeat_lanes(outer_ref, 2 * R, R)
        outer_stage(channel, column_ref, first_ref.at[channel], outer_ref, turn_ref, row_ref)
    sends = []
    size = 2 * R
    def forward_inner(group):
        every = slice(group * size, (group + 1) * size)
        inner_stage(mid_ref, row_ref, inner_ref, every)

    def multiply(group):
        for case in range(2 * group, 2 * group + 2):
            channel = case // 2
            for rows in chunks():
                here = slice(case * R + rows.start, case * R + rows.stop)
                real, imag = inner_parts(mid_ref, here)
                spec_real, spec_imag = spec_ref[channel, 0, rows, :], spec_ref[channel, 1, rows, :]
                put_row(
                    row_ref,
                    case * R,
                    rows,
                    real * spec_imag + imag * spec_real,
                    real * spec_real - imag * spec_imag,
                )

    def untwist(group):
        for case in range(2 * group, 2 * group + 2):
            for rows in chunks():
                here = slice(case * R + rows.start, case * R + rows.stop)
                imag, real = inner_parts(mid_ref, here)
                turn_real, turn_imag = turn_ref[0, rows, :], turn_ref[1, rows, :]
                put_column(last_ref, case, rows, real * turn_real + imag * turn_imag)
                below = slice(R + rows.start, R + rows.stop)
                put_column(last_ref, case, below, imag * turn_real - real * turn_imag)

    def backward_outer(group):
        result = dot(back_ref[...], last_ref[group])
        for rep in range(2):
            for half in range(2):
                lanes = slice(rep * R + half * 128, rep * R + half * 128 + 128)
                result_ref[group, rep, :, half * 16 : half * 16 + 16, :] = result[:, lanes].reshape(
                    blocks, 16, 128
                )
            sends.extend(
                start(
                    [
                        pltpu.make_async_copy(
                            result_ref.at[group, rep],
                            out_hbm.reshape(16, 2, 64, 128).at[:, rep, pl.ds(group * 32, 32), :],
                            out_sem.at[2 * group + rep],
                        )
                    ]
                )
            )

    stages = (forward_inner, multiply, forward_inner, untwist, backward_outer)
    groups = 2
    for step in range(len(stages) + groups - 1):
        for group in range(groups):
            if 0 <= step - group < len(stages):
                stages[step - group](group)
    finish(sends)


def convolve(moved, spec, turn, table):
    return pl.pallas_call(
        conv_kernel,
        in_specs=[HB] * 4,
        out_specs=HB,
        out_shape=jax.ShapeDtypeStruct((32, 64, 128), F32),
        scratch_shapes=[
            pltpu.VMEM(moved.shape, F32),
            pltpu.VMEM(spec.shape, F32),
            pltpu.VMEM(turn.shape, F32),
            pltpu.VMEM((2, 3 * R, 2 * R), BF),
            pltpu.VMEM((2, 2 * R, 2 * R), F32),
            pltpu.VMEM((4 * R, 9 * R), BF),
            pltpu.VMEM((4 * R, 3 * R), F32),
            pltpu.VMEM((2, 6 * R, 2 * R), BF),
            pltpu.VMEM((2, 2, 16, 32, 128), F32),
        ]
        + [pltpu.VMEM(*table_like) for table_like in TABLES]
        + [pltpu.SemaphoreType.DMA((9,)), pltpu.SemaphoreType.DMA((4,))],
        compiler_params=pltpu.CompilerParams(vmem_limit_bytes=60 << 20),
        name="convolve",
    )(moved, spec, turn, table)


def query_kernel(length_hbm, taps_ref, features_ref, out_ref, length_ref, column_ref, sem):
    group, width = out_ref.shape

    @pl.when(pl.program_id(0) == 0)
    def _():
        finish(start([pltpu.make_async_copy(length_hbm, length_ref, sem)]))
        taps_columns(taps_ref, column_ref)

    limit = length_ref[0] - lax.axis_index("seq") * width
    lane = lax.broadcasted_iota(jnp.int32, (8, width), 1)
    near = lane[:, 0:128]
    for sub in range(group // 8):
        rows = pl.ds(pl.multiple_of(pl.program_id(0) * group + sub * 8, 8), 8)
        column = column_ref[rows, :]
        here = features_ref[sub * 8 : sub * 8 + 8, :]
        t0, t1, t2 = (column[:, i : i + 1] for i in range(3))
        one = jnp.where(lane < 1, 0.0, pltpu.roll(here, 1, 1))
        two = jnp.where(lane < 2, 0.0, pltpu.roll(here, 2, 1))
        value = t0 * here + t1 * one + t2 * two
        out_ref[sub * 8 : sub * 8 + 8, :] = jnp.where(lane < limit, value, 0.0)


def query(lengths, short_filter, features):
    _, streams, channels, width = features.shape
    group = 16
    return pl.pallas_call(
        query_kernel,
        grid=(channels // group,),
        in_specs=[HB, VM, pl.BlockSpec((None, None, group, width), lambda i: (0, 0, i, 0))],
        out_specs=pl.BlockSpec((None, group, width), lambda i: (0, i, 0)),
        out_shape=jax.ShapeDtypeStruct((1, channels, width), F32),
        scratch_shapes=[
            pltpu.SMEM((1,), jnp.int32),
            pltpu.VMEM((channels, 128), F32),
            pltpu.SemaphoreType.DMA,
        ],
        compiler_params=pltpu.CompilerParams(vmem_limit_bytes=60 << 20),
        name="query",
    )(lengths, short_filter, features)


def mix_kernel(length_ref, tail_ref, query_hbm, back_ref, out_hbm, query_ref, sem):
    channels, width = query_ref.shape
    parts = 4
    group = channels // parts
    loads = []
    for part in range(parts):
        rows = pl.ds(group * part, group)
        loads += start([pltpu.make_async_copy(query_hbm.at[0, rows, :], query_ref.at[rows, :], sem.at[0, part])])
    limit = length_ref[0] - lax.axis_index("seq") * width
    near = lax.broadcasted_iota(jnp.int32, (8, 128), 1)
    sends = []
    for part in range(parts):
        finish(loads[part : part + 1])
        for sub in range(group // 8):
            channel = part * group + sub * 8
            here = slice(channel, channel + 8)
            tail = tail_ref[here, :]
            mend = jnp.where(near < 1, tail[:, 0:1], jnp.where(near < 2, tail[:, 1:2], 0.0))
            mend = jnp.where(near < limit, mend, 0.0)
            for tile in range(width // 128):
                row = channel * 32 + (tile % 2) * 16 + tile // 2
                lanes = slice(tile * 128, tile * 128 + 128)
                value = query_ref[here, lanes]
                if tile == 0:
                    value = value + mend
                query_ref[here, lanes] = value * back_ref[pl.ds(row, 8, stride=32), :]
        rows = pl.ds(group * part, group)
        sends += start([pltpu.make_async_copy(query_ref.at[rows, :], out_hbm.at[0, rows, :], sem.at[1, part])])
    finish(sends)


def mix(lengths, tail, query, returned):
    _, channels, width = query.shape
    return pl.pallas_call(
        mix_kernel,
        in_specs=[SM, VM, HB, VM],
        out_specs=HB,
        out_shape=jax.ShapeDtypeStruct(query.shape, F32),
        input_output_aliases={2: 0},
        scratch_shapes=[
            pltpu.VMEM((channels, width), F32),
            pltpu.SemaphoreType.DMA((2, 4)),
        ],
        compiler_params=pltpu.CompilerParams(vmem_limit_bytes=12 << 20),
        name="mix",
    )(lengths, tail, query, returned)


def exchange(blocks):
    return lax.all_to_all(blocks, ("seq", "x_lo"), split_axis=0, concat_axis=0, tiled=True)


def body(features, short_filter, long_filter, skip_gain, lengths):
    seq_dev = features.shape[3]
    n_seq = lax.axis_size("seq")
    table, turn = (jnp.asarray(t) for t in tables())
    other = lax.ppermute(long_filter, "x_lo", [(0, 1), (1, 0)])
    gated = gate(lengths, short_filter, features)
    gated, other = lax.optimization_barrier((gated, other))
    moved = exchange(gated.reshape(2 * n_seq, 2 * SPAN, 128))
    pair = pair_up(long_filter, other)
    parts = [pair] + [
        lax.ppermute(pair, "y", [(i, (i + away) % 4) for i in range(4)]) for away in range(1, 4)
    ]
    spec = filter_spectrum(skip_gain, parts, table, turn)
    convolved = convolve(moved, spec, turn, table)
    returned = exchange(convolved)
    far, last = features[0, 0, :, seq_dev - 2], features[0, 0, :, seq_dev - 1]
    one, two = short_filter[0, 1], short_filter[0, 2]
    over = jnp.stack([one * last + two * far, two * last], axis=1)
    tail = lax.ppermute(over, "seq", [(i, i + 1) for i in range(n_seq - 1)])
    gates = query(lengths, short_filter, features)
    return mix(lengths, tail, gates, returned.reshape(2 * n_seq * 64, 128))


def solution(mesh):
    devices = mesh.devices
    reps, seqs = devices.shape
    finer = Mesh(devices.reshape(reps // 2, 2, seqs), ("y", "x_lo", "seq"))
    rep = ("y", "x_lo")
    return jax.shard_map(
        body,
        mesh=finer,
        in_specs=(P(rep, None, None, "seq"), P(), P("seq", rep), P("seq"), P(rep)),
        out_specs=P(rep, None, "seq"),
        check_vma=False,
    )
```
